32 devices in a mesh: dp: 4 (over y, core), tp: 8 (over z, x).
Axes of the slice: x: 2, y: 2, z: 4, core: 2. Of those that a mesh axis runs over, the one named last changes fastest.
Arguments:
- teacher_partial: bfloat16 [8, 512, 4608], P('tp', 'dp'), may hold values from -5 to 5
- teacher_residual: bfloat16 [512, 4608], P(('dp', 'tp')), may hold values from -120 to 120
- post_gain: float32 [4608], replicated, may hold values from 0.5 to 1.5
- final_gain: float32 [4608], replicated, may hold values from 0.5 to 1.5
- teacher_head: bfloat16 [4608, 32768], P(None, ('dp', 'tp')), may hold values from -40 to 40
- student_hidden: bfloat16 [512, 3584], P(('dp', 'tp')), may hold values from -120 to 120
- student_gain: float32 [3584], replicated, may hold values from 0.5 to 1.5
- student_head: bfloat16 [3584, 32768], P(None, ('dp', 'tp')), may hold values from -40 to 40
- labels: int32 [512], P('dp'), may hold values from 0 to 32767
- lengths: int32 [4, 8], P('dp'), may hold values from 1 to 48, 96 in all within a row
Outputs:
- grad_hidden: float32 [512, 3584], P(('dp', 'tp'))
- token_loss: float32 [512], P(('dp', 'tp'))
The draws below stay inside these ranges and needn't reach their ends.
Inputs may be any that keep to these rules, and one draw needn't show every extreme that they name: `lengths`: group g's 8 sequences fill, in order, its first 96 rows; its remaining 128 - 96 rows are padding.
All inputs are finite; a program needn't handle non-finite values.
Results may differ from the reference program's by a relative error of at most 0.03.
Values may be sent and summed in bfloat16 or wider, within the bound.
No kernel may reach another device: no remote copies, remote signals or barrier semaphores. Data moves between devices by JAX's collectives and lax.ppermute only.
A program may use at most 128 MiB of HBM per device.

```python
import math
import jax
import jax.numpy as jnp
import numpy as np
from jax import lax

D_T = 4608
D_S = 3584
TOK_G = 128
NSEQ = 8
LIVE = 96
MOST = 48
GROUPS = 4
SPLITS = 8
TOKENS = 512
VOCAB = 32768


def hidden_draw(key, width, salt):
    values = jnp.clip(jax.random.normal(jax.random.fold_in(key, salt + 10), (TOKENS, width)), -6.0, 6.0)
    return values.astype(jnp.bfloat16)


def head_draw(key, width, salt):
    normal_part = jnp.clip(jax.random.normal(jax.random.fold_in(key, salt + 40), (width, VOCAB)), -6.0, 6.0)
    values = normal_part * (3.0 / math.sqrt(width))
    return values.astype(jnp.bfloat16)


def draw_teacher_residual(key, part):
    return hidden_draw(key, D_T, 4)


def draw_student_hidden(key, part):
    return hidden_draw(key, D_S, 5)


def draw_teacher_head(key, part):
    return head_draw(key, D_T, 4)


def draw_student_head(key, part):
    return head_draw(key, D_S, 5)


def plant(entries, own_key, low, largest):
    longest = entries.shape.index(max(entries.shape))
    spots = []
    for shift in (0, 1):
        where = [jax.random.randint(jax.random.fold_in(own_key, axis), (), 0, length) for axis, length in enumerate(entries.shape)]
        where[longest] = (where[longest] + shift) % entries.shape[longest]
        spots.append(tuple(where))
    return entries.at[spots[0]].set(low).at[spots[1]].set(largest)


def with_spikes(values, key, source, target, shards_of, factor):
    owner, partner = [(jnp.arange(values.shape[dim]) // (values.shape[dim] // shards_of)).reshape([-1 if axis == dim else 1 for axis in range(values.ndim)]) for dim in (source, target)]
    chosen = jax.random.permutation(key, shards_of)[partner]
    strong = (owner == chosen) | (owner == (partner + shards_of // 2) % shards_of)
    return jnp.where(strong, factor * values, values)


def block_scale(key, extent, split, low, largest):
    def one(position, shards_of):
        draws = jax.random.uniform(jax.random.fold_in(jax.random.fold_in(key, 6), position), (shards_of,), jnp.float32, low / len(split), largest / len(split))
        return jnp.repeat(jnp.exp(draws), extent[position] // shards_of).reshape((-1,) + (1,) * (len(extent) - position - 1))

    level = one(*split[0])
    for cut in split[1:]:
        level = level * one(*cut)
    return level


def split_up(number_of, total, most, lean):
    portions = [(1 << 20) // math.isqrt(grade ** lean) + 1 for grade in range(2, number_of + 1)]
    rest, holding = total - most - (number_of - 1), [1] * (number_of - 1)
    while rest > 0:
        free = [i for i in range(number_of - 1) if holding[i] < most]
        pool, remaining = sum([portions[i] for i in free]), rest
        for i in free:
            extra = min(most - holding[i], max(1, remaining * portions[i] // pool), rest)
            holding[i] = holding[i] + extra
            rest = rest - extra
    return np.array([most] + holding)


def ragged(rng, count, total, limit, skew):
    if count == 2:
        one = jax.random.randint(rng, (), max(1, total - limit), min(limit, total - 1) + 1)
        return jnp.stack([one, total - one])
    tallies = jnp.asarray(split_up(count, total, limit, skew), jnp.int32)
    twos = (count - 1) // 2
    donor, sink = tallies[1:1 + 2 * twos:2], tallies[2:2 + 2 * twos:2]
    slack = jnp.minimum(donor - 1, limit - sink)
    moved = jax.random.randint(jax.random.fold_in(rng, 1), (twos,), 0, 1 << 20) % (slack + 1)
    tallies = tallies.at[1:1 + 2 * twos:2].set(donor - moved).at[2:2 + 2 * twos:2].set(sink + moved)
    return tallies[jax.random.permutation(jax.random.fold_in(rng, 2), count)]


def bell_draw_with(rng, extent, scale, limit, split, heavy, held_as=jnp.bfloat16):
    values = scale * jax.random.normal(rng, extent, jnp.float32)
    if split:
        values = values * block_scale(rng, extent, split, -0.22, 0.18)
    return jnp.clip(with_spikes(values, jax.random.fold_in(rng, 3), *heavy), -limit, limit).astype(held_as)


def setup_inputs(seed: int = 0) -> dict:
    key_list = jax.random.split(jax.random.key(seed), 11)
    teacher_partial = bell_draw_with(key_list[0], (SPLITS, TOKENS, D_T), 0.25, 5.0, ((0, 8), (1, 4)), (0, 1, 8, 2.0))
    teacher_residual = draw_teacher_residual(jax.random.fold_in(key_list[10], 71), 0)
    post_gain = jnp.clip(1.0 + 0.1 * jax.random.normal(key_list[2], (D_T,), jnp.float32), 0.5, 1.5)
    final_gain = jnp.clip(1.0 + 0.1 * jax.random.normal(key_list[3], (D_T,), jnp.float32), 0.5, 1.5)
    teacher_head = draw_teacher_head(jax.random.fold_in(key_list[10], 71), 0)
    student_hidden = draw_student_hidden(jax.random.fold_in(key_list[10], 71), 0)
    student_gain = jnp.clip(1.0 + 0.1 * jax.random.normal(key_list[6], (D_S,), jnp.float32), 0.5, 1.5)
    student_head = draw_student_head(jax.random.fold_in(key_list[10], 71), 0)
    labels = plant(jax.random.randint(key_list[8], (TOKENS,), 0, VOCAB), jax.random.fold_in(key_list[8], 1), 0, VOCAB - 1).astype(jnp.int32)
    lengths = jax.vmap(lambda own: ragged(own, NSEQ, LIVE, MOST, 2))(jax.random.split(key_list[9], GROUPS)).reshape((GROUPS, NSEQ)).astype(jnp.int32)
    return {"teacher_partial": teacher_partial, "teacher_residual": teacher_residual, "post_gain": post_gain, "final_gain": final_gain, "teacher_head": teacher_head, "student_hidden": student_hidden, "student_gain": student_gain, "student_head": student_head, "labels": labels, "lengths": lengths}


EPS = 1e-06
BETA = 0.5
LOSS_SCALE = 1024.0

def norm_rows(values, gain):
    inverse = lax.rsqrt(lax.optimization_barrier(jnp.mean(values * values, axis=-1, keepdims=True)) + EPS)
    return (values * inverse * gain, inverse)

def token_weights(lengths, tok_rows):
    ends = jnp.cumsum(lengths, axis=1).astype(jnp.int32)
    starts = ends - lengths
    places = jnp.arange(tok_rows, dtype=jnp.int32)
    inside = (places[None, :, None] >= starts[:, None, :]) & (places[None, :, None] < ends[:, None, :])
    spans = lax.optimization_barrier(jnp.sum(jnp.where(inside, lengths[:, None, :], 0), axis=2))
    covered = lax.optimization_barrier(jnp.sum(inside.astype(jnp.int32), axis=2))
    return covered.astype(jnp.float32) / jnp.maximum(spans, 1).astype(jnp.float32)

def reference(teacher_partial, teacher_residual, post_gain, final_gain, teacher_head, student_hidden, student_gain, student_head, labels, lengths):
    mlp_sum = lax.optimization_barrier(jnp.sum(teacher_partial, axis=0, dtype=jnp.float32))
    post, unused = norm_rows(mlp_sum, post_gain)
    final = teacher_residual.astype(jnp.float32) + post
    teacher_norm = norm_rows(final, final_gain)[0].astype(jnp.bfloat16)
    student_f = student_hidden.astype(jnp.float32)
    student_scaled, inverse = norm_rows(student_f, student_gain)
    student_norm = student_scaled.astype(jnp.bfloat16)
    weight = token_weights(lengths, TOK_G).reshape(-1)
    t_logits = jnp.dot(teacher_norm.astype(jnp.float32), teacher_head.astype(jnp.float32), preferred_element_type=jnp.float32)
    s_logits = jnp.dot(student_norm.astype(jnp.float32), student_head.astype(jnp.float32), preferred_element_type=jnp.float32)
    t_max = lax.optimization_barrier(jnp.max(t_logits, axis=1))
    t_log = t_max + jnp.log(lax.optimization_barrier(jnp.sum(jnp.exp(t_logits - t_max[:, None]), axis=1)))
    s_max = lax.optimization_barrier(jnp.max(s_logits, axis=1))
    s_log = s_max + jnp.log(lax.optimization_barrier(jnp.sum(jnp.exp(s_logits - s_max[:, None]), axis=1)))
    t_logp = t_logits - t_log[:, None]
    s_logp = s_logits - s_log[:, None]
    t_prob = jnp.exp(t_logp)
    s_prob = jnp.exp(s_logp)
    divergence = lax.optimization_barrier(jnp.sum(t_prob * (t_logp - s_logp), axis=1))
    columns = jnp.arange(VOCAB, dtype=jnp.int32)
    hit = labels[:, None] == columns[None, :]
    label_value = lax.optimization_barrier(jnp.sum(jnp.where(hit, s_logits, 0.0), axis=1))
    label_term = s_log - label_value
    token_loss = jnp.where(weight > 0, divergence + BETA * label_term, 0.0)
    scale = (LOSS_SCALE * weight)[:, None]
    logit_grad = (scale * ((1.0 + BETA) * s_prob - t_prob - BETA * hit.astype(jnp.float32))).astype(jnp.bfloat16)
    norm_grad = jnp.dot(logit_grad.astype(jnp.float32), student_head.T.astype(jnp.float32), preferred_element_type=jnp.float32)
    scaled = norm_grad * student_gain
    inner = lax.optimization_barrier(jnp.mean(scaled * student_f, axis=1, keepdims=True))
    grad_hidden = inverse * scaled - student_f * (inverse * inverse * inverse) * inner
    return (grad_hidden, token_loss)
```

```python
import jax
import jax.numpy as jnp
from jax import lax
from jax.sharding import PartitionSpec as P

EPS = 1e-06
BETA = 0.5
LOSS_SCALE = 1024.0
LIVE = 96
F32 = jnp.float32
BF16 = jnp.bfloat16
AXES = ("dp", "tp")


class Grid:
    def __init__(self, dp, tp, share):
        assert dp == 4 and tp % 2 == 0
        self.tp, self.depth = tp, tp // 2
        self.live = LIVE // (2 * share)
        assert self.live * 2 * share == LIVE
        dp_at, tp_at = lax.axis_index("dp"), lax.axis_index("tp")
        self.y, self.c = dp_at // 2, dp_at % 2
        self.z, self.x = tp_at // 2, tp_at % 2

    def send(self, value, a=0, b=0, k=0, d=0, source=None, target=None):
        pairs = []
        for dp_at in range(4):
            for tp_at in range(self.tp):
                z = tp_at // 2
                if source is not None and z >= source:
                    continue
                if target is not None and (z ^ k) >= target:
                    continue
                to = (dp_at ^ (2 * a + b)) * self.tp + (tp_at ^ (2 * k + d))
                pairs.append((dp_at * self.tp + tp_at, to))
        return lax.ppermute(value, AXES, pairs)


def pick(pieces, index):
    bit = 0
    while len(pieces) > 1:
        high = (index >> bit) & 1
        pieces = [jnp.where(high == 1, pieces[i + 1], pieces[i]) for i in range(0, len(pieces), 2)]
        bit += 1
    return pieces[0]


def norm_rows(values, gain):
    inverse = lax.rsqrt(jnp.mean(values * values, axis=-1, keepdims=True) + EPS)
    return (values * inverse * gain, inverse)


def gather_depth(grid, rows):
    pieces = [rows] + [grid.send(rows, k=k, source=grid.live) for k in range(1, grid.depth)]
    return jnp.concatenate([pick(pieces, grid.z ^ j) for j in range(grid.live)], axis=0)


def gather_rows(grid, rows):
    half = rows.shape[1] // 2
    own = gather_depth(grid, rows)
    by_x = grid.send(own, d=1)
    by_y = grid.send(own, a=1)
    own_c = grid.send(own, b=1)
    far = jnp.concatenate(
        [grid.send(by_x[:, :half], a=1), grid.send(by_y[:, half:], d=1)], axis=1
    )
    by_x_c = grid.send(by_x, b=1)
    by_y_c = grid.send(by_y, b=1)
    far_c = grid.send(far, b=1)
    return jnp.concatenate([own, by_x, own_c, by_x_c, by_y, far, by_y_c, far_c], axis=0)


def row_weights(lengths, tok_rows):
    ends = jnp.cumsum(lengths, axis=1)
    starts = ends - lengths
    places = jnp.arange(tok_rows, dtype=jnp.int32)
    inside = (places[None, :, None] >= starts[:, None, :]) & (
        places[None, :, None] < ends[:, None, :]
    )
    spans = jnp.sum(jnp.where(inside, lengths[:, None, :], 0), axis=2)
    covered = jnp.sum(inside.astype(jnp.int32), axis=2)
    return covered.astype(F32) / jnp.maximum(spans, 1).astype(F32)


def exchange(grid, stats, merge):
    def turned(value, axes):
        return jnp.flip(value, axes)

    stats = merge([stats, turned(grid.send(stats, b=1), (2,))])
    stats = merge(
        [
            stats,
            turned(grid.send(stats, d=1), (3,)),
            turned(grid.send(stats, a=1), (1,)),
            turned(grid.send(stats, a=1, d=1), (1, 3)),
        ]
    )
    return merge([stats] + [grid.send(stats, k=k) for k in range(1, grid.depth)])


def merge_with_max(parts):
    top = parts[0][0]
    for part in parts[1:]:
        top = jnp.maximum(top, part[0])
    rest = 0.0
    for part in parts:
        rest = rest + jnp.exp(part[0] - top)[None] * part[1:]
    return jnp.concatenate([top[None], rest], axis=0)


def merge_student(parts):
    both = merge_with_max([part[:2] for part in parts])
    label = sum([part[2:] for part in parts[1:]], parts[0][2:])
    return jnp.concatenate([both, label], axis=0)


def shards(
    teacher_partial,
    teacher_residual,
    post_gain,
    final_gain,
    teacher_head,
    student_hidden,
    student_gain,
    student_head,
    labels,
    lengths,
):
    share, width_t = teacher_residual.shape
    width_s = student_hidden.shape[1]
    tok_rows = labels.shape[0]
    nseq = lengths.shape[1]
    grid = Grid(lax.axis_size("dp"), lax.axis_size("tp"), share)
    live = grid.live

    parts = teacher_partial[0, :LIVE].reshape(live, 2, share, width_t)
    kept = lax.dynamic_index_in_dim(parts, grid.x, 1, keepdims=False)
    given = lax.dynamic_index_in_dim(parts, 1 - grid.x, 1, keepdims=False)
    pair = kept.astype(F32) + grid.send(given, d=1).astype(F32)
    pair_low = pair.astype(BF16)
    at = jnp.minimum(grid.z, live - 1)
    mlp_sum = lax.dynamic_index_in_dim(pair, at, 0, keepdims=False)
    for k in range(1, grid.depth):
        to = jnp.minimum(grid.z ^ k, live - 1)
        chunk = lax.dynamic_index_in_dim(pair_low, to, 0, keepdims=False)
        mlp_sum = mlp_sum + grid.send(chunk, k=k, target=live).astype(F32)

    student_f = student_hidden.astype(F32)
    student_scaled, inverse = norm_rows(student_f, student_gain)
    whole_s = gather_rows(grid, student_scaled.astype(BF16))

    ints = jnp.concatenate([labels, lengths[0]])[None]
    ints = jnp.concatenate([ints, grid.send(ints, b=1)], axis=0)
    ints = jnp.concatenate([ints, grid.send(ints, a=1)], axis=0)

    def by_row(value):
        value = value[:, :LIVE].reshape(4, live, 2, share)
        value = jnp.moveaxis(value, 2, 1)
        value = jnp.where(grid.x == 1, jnp.flip(value, 1), value)
        return value.reshape(2, 2, 2, live * share)

    label_rows = by_row(ints[:, :tok_rows])
    weight_rows = by_row(row_weights(ints[:, tok_rows : tok_rows + nseq], tok_rows))

    post, unused = norm_rows(mlp_sum, post_gain)
    final = teacher_residual.astype(F32) + post
    teacher_norm = norm_rows(final, final_gain)[0].astype(BF16)
    whole_t = gather_rows(grid, teacher_norm)

    rows = whole_s.shape[0]
    shape = label_rows.shape
    vocab_dev = student_head.shape[1]
    position = lax.axis_index("dp") * lax.axis_size("tp") + lax.axis_index("tp")
    columns = position * vocab_dev + jnp.arange(vocab_dev, dtype=jnp.int32)
    hit = label_rows.reshape(rows)[:, None] == columns[None, :]

    s_logits = jnp.dot(whole_s, student_head, preferred_element_type=F32)
    s_local = jnp.max(s_logits, axis=1)
    s_sum = jnp.sum(jnp.exp(s_logits - s_local[:, None]), axis=1)
    s_label = jnp.sum(jnp.where(hit, s_logits, 0.0), axis=1)
    s_stats = exchange(
        grid, jnp.stack([s_local, s_sum, s_label]).reshape((3,) + shape), merge_student
    )

    t_logits = jnp.dot(whole_t, teacher_head, preferred_element_type=F32)
    t_local = jnp.max(t_logits, axis=1)
    t_exp = jnp.exp(t_logits - t_local[:, None])
    t_sum = jnp.sum(t_exp, axis=1)
    t_mix = jnp.sum(t_exp * (t_logits - s_logits), axis=1)
    t_stats = exchange(
        grid, jnp.stack([t_local, t_sum, t_mix]).reshape((3,) + shape), merge_with_max
    )

    s_max, s_total, label_value = s_stats
    t_max, t_total, t_cross = t_stats
    t_log = t_max + jnp.log(t_total)
    s_log = s_max + jnp.log(s_total)
    divergence = t_cross / t_total - t_log + s_log
    label_term = s_log - label_value
    row_loss = jnp.where(weight_rows > 0, divergence + BETA * label_term, 0.0)

    def column(value):
        return value.reshape(rows)[:, None]

    t_prob = jnp.exp(t_logits - column(t_max)) / column(t_total)
    s_prob = jnp.exp(s_logits - column(s_max)) / column(s_total)
    scale = LOSS_SCALE * column(weight_rows)
    logit_grad = (scale * ((1.0 + BETA) * s_prob - t_prob - BETA * hit.astype(F32))).astype(BF16)
    partial = lax.dot_general(
        logit_grad, student_head, (((1,), (1,)), ((), ())), preferred_element_type=F32
    ).reshape(2, 2, 2, live * share, width_s)

    half = width_s // 2
    total = partial[:, 0] + grid.send(partial[:, 1].astype(BF16), b=1).astype(F32)
    far = total[1, 1].astype(BF16)
    got_x = grid.send(far[:, :half], d=1).astype(F32)
    got_y = grid.send(far[:, half:], a=1).astype(F32)
    to_y = jnp.concatenate([total[1, 0, :, :half] + got_x, total[1, 0, :, half:]], axis=1)
    to_x = jnp.concatenate([total[0, 1, :, :half], total[0, 1, :, half:] + got_y], axis=1)
    mine = (
        total[0, 0]
        + grid.send(to_y.astype(BF16), a=1).astype(F32)
        + grid.send(to_x.astype(BF16), d=1).astype(F32)
    ).reshape(live, share, width_s)
    mine_low = mine.astype(BF16)
    summed = lax.dynamic_index_in_dim(mine, at, 0, keepdims=False)
    for k in range(1, grid.depth):
        to = jnp.minimum(grid.z ^ k, live - 1)
        chunk = lax.dynamic_index_in_dim(mine_low, to, 0, keepdims=False)
        summed = summed + grid.send(chunk, k=k, target=live).astype(F32)

    scaled = summed * student_gain
    inner = jnp.mean(scaled * student_f, axis=1, keepdims=True)
    grad_hidden = inverse * scaled - student_f * (inverse * inverse * inverse) * inner
    own = grid.z < live
    grad_hidden = jnp.where(own, grad_hidden, 0.0)
    own_loss = lax.dynamic_slice_in_dim(row_loss[0, 0, 0], at * share, share, 0)
    return (grad_hidden, jnp.where(own, own_loss, 0.0))


def solution(mesh):
    placed = (
        P("tp", "dp", None),
        P(("dp", "tp"), None),
        P(),
        P(),
        P(None, ("dp", "tp")),
        P(("dp", "tp"), None),
        P(),
        P(None, ("dp", "tp")),
        P("dp"),
        P("dp", None),
    )
    return jax.shard_map(
        shards,
        mesh=mesh,
        in_specs=placed,
        out_specs=(P(("dp", "tp"), None), P(("dp", "tp"))),
        check_vma=False,
    )
```

```python
import functools

import jax
import jax.numpy as jnp
from jax import lax
from jax.experimental import pallas as pl
from jax.experimental.pallas import tpu as pltpu
from jax.sharding import PartitionSpec as P


EPS = 1e-06
BETA = 0.5
LOSS_SCALE = 1024.0
LIVE = 96
F32 = jnp.float32
BF16 = jnp.bfloat16
AXES = ("dp", "tp")


class Grid:
    def __init__(self, dp, tp, share):
        assert dp == 4 and tp % 2 == 0
        self.tp, self.depth = tp, tp // 2
        self.live = LIVE // (2 * share)
        assert self.live * 2 * share == LIVE
        dp_at, tp_at = lax.axis_index("dp"), lax.axis_index("tp")
        self.y, self.c = dp_at // 2, dp_at % 2
        self.z, self.x = tp_at // 2, tp_at % 2
        self.tiled = share % 16 == 0
        self.ids = jnp.stack([self.y, self.c, self.z, self.x, dp_at * tp + tp_at])

    def send(self, value, a=0, b=0, k=0, d=0, source=None, target=None):
        pairs = []
        for dp_at in range(4):
            for tp_at in range(self.tp):
                z = tp_at // 2
                if source is not None and z >= source:
                    continue
                if target is not None and (z ^ k) >= target:
                    continue
                to = (dp_at ^ (2 * a + b)) * self.tp + (tp_at ^ (2 * k + d))
                pairs.append((dp_at * self.tp + tp_at, to))
        return lax.ppermute(value, AXES, pairs)


def pick(pieces, index):
    bit = 0
    while len(pieces) > 1:
        high = (index >> bit) & 1
        pieces = [jnp.where(high == 1, pieces[i + 1], pieces[i]) for i in range(0, len(pieces), 2)]
        bit += 1
    return pieces[0]


def norm_rows(values, gain):
    inverse = lax.rsqrt(jnp.mean(values * values, axis=-1, keepdims=True) + EPS)
    return (values * inverse * gain, inverse)


VMEM = pl.BlockSpec(memory_space=pltpu.VMEM)
SMEM = pl.BlockSpec(memory_space=pltpu.SMEM)
shape_of = pltpu.VMEM
MIB = 1 << 20


def call(kernel, ids, args, outs, scratch, mib):
    args = [pltpu.with_memory_space_constraint(arg, pltpu.VMEM) for arg in args]
    return pl.pallas_call(
        kernel,
        out_shape=outs,
        in_specs=[SMEM] + [VMEM] * len(args),
        out_specs=[VMEM] * len(outs),
        scratch_shapes=scratch,
        compiler_params=pltpu.CompilerParams(vmem_limit_bytes=mib * MIB),
    )(ids, *args)


def pick_kernel(live, ids, *refs):
    pieces, out = refs[:-1], refs[-1]
    share = pieces[0].shape[0]
    for j in range(live):
        for k, piece in enumerate(pieces):

            @pl.when((ids[2] ^ j) == k)
            def _(j=j, piece=piece):
                out[j * share : (j + 1) * share, :] = piece[...]


def pair_kernel(live, ids, partial, other, own, *lows):
    share = own.shape[0]

    def chunk(slot):
        slot = jnp.minimum(slot, live - 1)
        at = pl.multiple_of((2 * slot + ids[3]) * share, share)
        return partial[0, pl.ds(at, share), :].astype(F32) + other[slot].astype(F32)

    own[...] = chunk(ids[2])
    for k, low in enumerate(lows, 1):
        low[...] = chunk(ids[2] ^ k).astype(BF16)


def norm_kernel(ids, *refs):
    own, others = refs[0], refs[1:-4]
    residual, post_gain, final_gain, out = refs[-4:]
    total = own[...]
    for other in others:
        total = total + other[...].astype(F32)
    post, _ = norm_rows(total, post_gain[...])
    final = residual[...].astype(F32) + post
    out[...] = norm_rows(final, final_gain[...])[0].astype(BF16)


def gather_depth(grid, rows):
    pieces = [rows] + [grid.send(rows, k=k, source=grid.live) for k in range(1, grid.depth)]
    if not grid.tiled:
        return jnp.concatenate([pick(pieces, grid.z ^ j) for j in range(grid.live)], axis=0)
    return call(
        functools.partial(pick_kernel, grid.live),
        grid.ids,
        pieces,
        [shape_of((grid.live * rows.shape[0], rows.shape[1]), rows.dtype)],
        [],
        4,
    )[0]


def gather_plane(grid, own):
    by_x = grid.send(own, d=1)
    by_y = grid.send(own, a=1)
    far = grid.send(own, a=1, d=1)
    own_c = grid.send(own, b=1)
    by_x_c = grid.send(by_x, b=1)
    by_y_c = grid.send(by_y, b=1)
    far_c = grid.send(far, b=1)
    return jnp.concatenate([own, by_x, own_c, by_x_c, by_y, far, by_y_c, far_c], axis=0)


def reduce_rows(grid, low, other, share):
    total = low + other.astype(F32)
    low = total.astype(BF16)
    by_x = grid.send(low[0, 1], d=1)
    by_y = grid.send(low[1, 0], a=1)
    far = grid.send(low[1, 1], a=1, d=1)
    mine = total[0, 0] + by_x.astype(F32) + by_y.astype(F32) + far.astype(F32)
    mine = mine.reshape(grid.live, share, total.shape[-1])
    mine_low = mine.astype(BF16)
    summed = lax.dynamic_index_in_dim(
        mine, jnp.minimum(grid.z, grid.live - 1), 0, keepdims=False
    )
    for k in range(1, grid.depth):
        to = jnp.minimum(grid.z ^ k, grid.live - 1)
        chunk = lax.dynamic_index_in_dim(mine_low, to, 0, keepdims=False)
        chunk = grid.send(chunk, k=k, target=grid.live)
        summed = summed + chunk.astype(F32)
    return summed


def row_weights(lengths, tok_rows):
    ends = jnp.cumsum(lengths, axis=1)
    starts = ends - lengths
    places = jnp.arange(tok_rows, dtype=jnp.int32)
    inside = (places[None, :, None] >= starts[:, None, :]) & (
        places[None, :, None] < ends[:, None, :]
    )
    spans = jnp.sum(jnp.where(inside, lengths[:, None, :], 0), axis=2)
    covered = jnp.sum(inside.astype(jnp.int32), axis=2)
    return covered.astype(F32) / jnp.maximum(spans, 1).astype(F32)


def turn(grid, value):
    for axis, at in ((1, grid.y), (2, grid.c), (3, grid.x)):
        value = jnp.where(at == 1, jnp.flip(value, axis), value)
    return value


def exchange(grid, stats):
    devices = 4 * grid.tp
    flat = turn(grid, stats).reshape(-1)
    sent = jnp.broadcast_to(flat[None], (devices, flat.shape[0])).reshape(-1)
    got = lax.all_to_all(sent, AXES, 0, 0, tiled=True)
    return got.reshape((devices,) + stats.shape)


def join_logs(logs):
    top = jnp.max(logs, axis=0)
    return top + jnp.log(jnp.sum(jnp.exp(logs - top[None]), axis=0))


def shards(
    teacher_partial,
    teacher_residual,
    post_gain,
    final_gain,
    teacher_head,
    student_hidden,
    student_gain,
    student_head,
    labels,
    lengths,
):
    share, width_t = teacher_residual.shape
    width_s = student_hidden.shape[1]
    tok_rows = labels.shape[0]
    nseq = lengths.shape[1]
    grid = Grid(lax.axis_size("dp"), lax.axis_size("tp"), share)
    live = grid.live

    parts = teacher_partial[0, :LIVE].reshape(live, 2, share, width_t)
    given = lax.dynamic_index_in_dim(parts, 1 - grid.x, 1, keepdims=False)
    other = grid.send(given, d=1)
    at = jnp.minimum(grid.z, live - 1)
    ks = range(1, grid.depth)
    if grid.tiled:
        own, *lows = call(
            functools.partial(pair_kernel, live),
            grid.ids,
            [teacher_partial, other],
            [shape_of((share, width_t), F32)] + [shape_of((share, width_t), BF16) for k in ks],
            [],
            4,
        )
    else:
        kept = lax.dynamic_index_in_dim(parts, grid.x, 1, keepdims=False)
        pair = kept.astype(F32) + other.astype(F32)
        own = lax.dynamic_index_in_dim(pair, at, 0, keepdims=False)
        lows = [
            lax.dynamic_index_in_dim(
                pair, jnp.minimum(grid.z ^ k, live - 1), 0, keepdims=False
            ).astype(BF16)
            for k in ks
        ]
    others = [grid.send(low, k=k, target=live) for k, low in zip(ks, lows)]

    student_f = student_hidden.astype(F32)
    student_scaled, inverse = norm_rows(student_f, student_gain)
    student_norm = student_scaled.astype(BF16)
    own_s = gather_depth(grid, student_norm)
    whole_s = gather_plane(grid, own_s)

    ints = jnp.concatenate([labels, lengths[0]])[None]
    ints = jnp.concatenate([ints, grid.send(ints, b=1)], axis=0)
    ints = jnp.concatenate([ints, grid.send(ints, a=1)], axis=0)

    def by_row(value):
        value = value[:, :LIVE].reshape(4, live, 2, share)
        value = jnp.moveaxis(value, 2, 1)
        value = jnp.where(grid.x == 1, jnp.flip(value, 1), value)
        return value.reshape(2, 2, 2, live * share)

    label_rows = by_row(ints[:, :tok_rows])
    weight_rows = by_row(row_weights(ints[:, tok_rows : tok_rows + nseq], tok_rows))

    if grid.tiled:
        teacher_norm = call(
            norm_kernel,
            grid.ids,
            [own, *others, teacher_residual, post_gain[None], final_gain[None]],
            [shape_of((share, width_t), BF16)],
            [],
            4,
        )[0]
    else:
        mlp_sum = own
        for other in others:
            mlp_sum = mlp_sum + other.astype(F32)
        post, _ = norm_rows(mlp_sum, post_gain)
        final = teacher_residual.astype(F32) + post
        teacher_norm = norm_rows(final, final_gain)[0].astype(BF16)
    own_t = gather_depth(grid, teacher_norm)
    whole_t = gather_plane(grid, own_t)

    rows = whole_s.shape[0]
    shape = label_rows.shape
    vocab_dev = student_head.shape[1]
    position = lax.axis_index("dp") * lax.axis_size("tp") + lax.axis_index("tp")
    columns = position * vocab_dev + jnp.arange(vocab_dev, dtype=jnp.int32)
    hit = label_rows.reshape(rows)[:, None] == columns[None, :]

    s_logits = jnp.dot(whole_s, student_head, preferred_element_type=F32)
    s_top = jnp.max(s_logits, axis=1)
    s_own = s_top + jnp.log(jnp.sum(jnp.exp(s_logits - s_top[:, None]), axis=1))
    s_label = jnp.sum(jnp.where(hit, s_logits, 0.0), axis=1)

    t_logits = jnp.dot(whole_t, teacher_head, preferred_element_type=F32)
    t_top = jnp.max(t_logits, axis=1)
    t_exp = jnp.exp(t_logits - t_top[:, None])
    t_sum = jnp.sum(t_exp, axis=1)
    t_mix = jnp.sum(t_exp * (t_logits - s_logits), axis=1) / t_sum
    t_own = t_top + jnp.log(t_sum)

    stats = exchange(grid, jnp.stack([t_own, t_mix, s_own, s_label]).reshape((4,) + shape))
    t_log = join_logs(stats[:, 0])
    t_cross = jnp.sum(jnp.exp(stats[:, 0] - t_log[None]) * stats[:, 1], axis=0)
    s_log = join_logs(stats[:, 2])
    label_value = jnp.sum(stats[:, 3], axis=0)
    t_log, t_cross, s_log, label_value = turn(
        grid, jnp.stack([t_log, t_cross, s_log, label_value])
    )
    divergence = t_cross - t_log + s_log
    label_term = s_log - label_value
    row_loss = jnp.where(weight_rows > 0, divergence + BETA * label_term, 0.0)

    def column(value):
        return value.reshape(rows)[:, None]

    t_prob = jnp.exp(t_logits - column(t_log))
    s_prob = jnp.exp(s_logits - column(s_log))
    scale = LOSS_SCALE * column(weight_rows)
    logit_grad = (scale * ((1.0 + BETA) * s_prob - t_prob - BETA * hit.astype(F32))).astype(BF16)
    partial = lax.dot_general(
        logit_grad, student_head, (((1,), (1,)), ((), ())), preferred_element_type=F32
    ).reshape(2, 2, 2, live * share, width_s)

    other = grid.send(partial[:, 1].astype(BF16), b=1)
    summed = reduce_rows(grid, partial[:, 0], other, share)

    scaled = summed * student_gain
    inner = jnp.mean(scaled * student_f, axis=1, keepdims=True)
    grad_hidden = inverse * scaled - student_f * (inverse * inverse * inverse) * inner
    own = grid.z < live
    grad_hidden = jnp.where(own, grad_hidden, 0.0)
    own_loss = lax.dynamic_slice_in_dim(row_loss[0, 0, 0], at * share, share, 0)
    return (grad_hidden, jnp.where(own, own_loss, 0.0))


def solution(mesh):
    placed = (
        P("tp", "dp", None),
        P(("dp", "tp"), None),
        P(),
        P(),
        P(None, ("dp", "tp")),
        P(("dp", "tp"), None),
        P(),
        P(None, ("dp", "tp")),
        P("dp"),
        P("dp", None),
    )
    return jax.shard_map(
        shards,
        mesh=mesh,
        in_specs=placed,
        out_specs=(P(("dp", "tp"), None), P(("dp", "tp"))),
        check_vma=False,
    )
```

```python
import functools

import jax
import jax.numpy as jnp
from jax import lax
from jax.experimental import pallas as pl
from jax.experimental.pallas import tpu as pltpu
from jax.sharding import PartitionSpec as P


EPS = 1e-06
BETA = 0.5
LOSS_SCALE = 1024.0
LIVE = 96
F32 = jnp.float32
BF16 = jnp.bfloat16
AXES = ("dp", "tp")


class Grid:
    def __init__(self, dp, tp, share):
        assert dp == 4 and tp % 2 == 0
        self.tp, self.depth = tp, tp // 2
        self.live = LIVE // (2 * share)
        assert self.live * 2 * share == LIVE
        dp_at, tp_at = lax.axis_index("dp"), lax.axis_index("tp")
        self.y, self.c = dp_at // 2, dp_at % 2
        self.z, self.x = tp_at // 2, tp_at % 2
        self.tiled = share % 16 == 0
        self.ids = jnp.stack([self.y, self.c, self.z, self.x, dp_at * tp + tp_at])

    def send(self, value, a=0, b=0, k=0, d=0, source=None, target=None):
        pairs = []
        for dp_at in range(4):
            for tp_at in range(self.tp):
                z = tp_at // 2
                if source is not None and z >= source:
                    continue
                if target is not None and (z ^ k) >= target:
                    continue
                to = (dp_at ^ (2 * a + b)) * self.tp + (tp_at ^ (2 * k + d))
                pairs.append((dp_at * self.tp + tp_at, to))
        return lax.ppermute(value, AXES, pairs)


def pick(pieces, index):
    bit = 0
    while len(pieces) > 1:
        high = (index >> bit) & 1
        pieces = [jnp.where(high == 1, pieces[i + 1], pieces[i]) for i in range(0, len(pieces), 2)]
        bit += 1
    return pieces[0]


def norm_rows(values, gain):
    inverse = lax.rsqrt(jnp.mean(values * values, axis=-1, keepdims=True) + EPS)
    return (values * inverse * gain, inverse)


VMEM = pl.BlockSpec(memory_space=pltpu.VMEM)
SMEM = pl.BlockSpec(memory_space=pltpu.SMEM)
shape_of = pltpu.VMEM
MIB = 1 << 20


def call(kernel, ids, args, outs, scratch, mib, far=()):
    args = [pltpu.with_memory_space_constraint(arg, pltpu.VMEM) for arg in args]
    far = [pltpu.with_memory_space_constraint(arg, pltpu.HBM) for arg in far]
    return pl.pallas_call(
        kernel,
        out_shape=outs,
        in_specs=[SMEM] + [VMEM] * len(args) + [pl.BlockSpec(memory_space=pltpu.HBM)] * len(far),
        out_specs=[VMEM] * len(outs),
        scratch_shapes=scratch,
        compiler_params=pltpu.CompilerParams(vmem_limit_bytes=mib * MIB),
    )(ids, *args, *far)


def pick_kernel(live, ids, *refs):
    pieces, out = refs[:-1], refs[-1]
    share = pieces[0].shape[0]
    for j in range(live):
        for k, piece in enumerate(pieces):

            @pl.when((ids[2] ^ j) == k)
            def _(j=j, piece=piece):
                out[j * share : (j + 1) * share, :] = piece[...]


def pair_kernel(live, ids, partial, other, own, *lows):
    share = own.shape[0]

    def chunk(slot):
        slot = jnp.minimum(slot, live - 1)
        at = pl.multiple_of((2 * slot + ids[3]) * share, share)
        return partial[0, pl.ds(at, share), :].astype(F32) + other[slot].astype(F32)

    own[...] = chunk(ids[2])
    for k, low in enumerate(lows, 1):
        low[...] = chunk(ids[2] ^ k).astype(BF16)


def norm_kernel(ids, *refs):
    own, others = refs[0], refs[1:-4]
    residual, post_gain, final_gain, out = refs[-4:]
    total = own[...]
    for other in others:
        total = total + other[...].astype(F32)
    post, _ = norm_rows(total, post_gain[...])
    final = residual[...].astype(F32) + post
    out[...] = norm_rows(final, final_gain[...])[0].astype(BF16)


def gather_depth(grid, rows):
    pieces = [rows] + [grid.send(rows, k=k, source=grid.live) for k in range(1, grid.depth)]
    if not grid.tiled:
        return jnp.concatenate([pick(pieces, grid.z ^ j) for j in range(grid.live)], axis=0)
    return call(
        functools.partial(pick_kernel, grid.live),
        grid.ids,
        pieces,
        [shape_of((grid.live * rows.shape[0], rows.shape[1]), rows.dtype)],
        [],
        4,
    )[0]


def gather_plane(grid, own):
    by_x = grid.send(own, d=1)
    by_y = grid.send(own, a=1)
    far = grid.send(own, a=1, d=1)
    own_c = grid.send(own, b=1)
    by_x_c = grid.send(by_x, b=1)
    by_y_c = grid.send(by_y, b=1)
    far_c = grid.send(far, b=1)
    return jnp.concatenate([own, by_x, own_c, by_x_c, by_y, far, by_y_c, far_c], axis=0)


def lane(shape):
    return lax.broadcasted_iota(jnp.int32, shape, 1)


def own_place(ids):
    return ids[0] * 4 + ids[1] * 2 + ids[3]


def block_rows(number, rows):
    return pl.ds(pl.multiple_of(number * rows, rows), rows)


def student_kernel(ids, logits, labels, cols):
    vocab = logits.shape[1]
    rows = logits.shape[0] // 8
    mine = own_place(ids)

    def step(r, carry):
        here = block_rows(r, rows)
        block = logits[here, :]
        top = jnp.max(block, axis=1, keepdims=True)
        log = top + jnp.log(jnp.sum(jnp.exp(block - top), axis=1, keepdims=True))
        hit = labels[here, :] - ids[4] * vocab == lane(block.shape)
        value = jnp.sum(jnp.where(hit, block, 0.0), axis=1, keepdims=True)
        places = lane((rows, 128))
        cols[block_rows(mine ^ r, rows), :] = jnp.where(
            places == 1, log, jnp.where(places == 3, value, 0.0)
        )
        return carry

    lax.fori_loop(0, 8, step, 0)


def teacher_kernel(ids, logits, s_logits, s_cols, sent, cols):
    rows = logits.shape[0] // 8
    mine = own_place(ids)

    def step(r, carry):
        here = block_rows(r, rows)
        block = logits[here, :]
        top = jnp.max(block, axis=1, keepdims=True)
        weights = jnp.exp(block - top)
        total = jnp.sum(weights, axis=1, keepdims=True)
        mix = jnp.sum(weights * (block - s_logits[here, :]), axis=1, keepdims=True) / total
        places = lane((rows, 128))
        log = top + jnp.log(total)
        there = block_rows(mine ^ r, rows)
        cols[there, :] = jnp.where(
            places == 0, log, jnp.where(places == 2, mix, s_cols[there, :])
        )
        return carry

    lax.fori_loop(0, 8, step, 0, unroll=4)
    turned = cols[...].T
    message = jnp.concatenate([turned[n : n + 1, :] for n in range(4)], axis=1)
    for d in range(sent.shape[0]):
        sent[d] = message


def joined(got, rows):
    every = [got[d][:, : 2 * rows] for d in range(got.shape[0])]
    top = functools.reduce(jnp.maximum, every)
    return top + jnp.log(sum([jnp.exp(part - top) for part in every[1:]], jnp.exp(every[0] - top)))


def product_into(out, grads, head):
    height = head.shape[0] // 4

    def step(n, carry):
        here = block_rows(n, height)
        value = lax.dot_general(
            grads[...], head[here, :], (((1,), (1,)), ((), ())), preferred_element_type=F32
        )
        out[:, here] = value.astype(out.dtype)
        return carry

    lax.fori_loop(0, 4, step, 0)


def given_kernel(
    ids, got, labels, scale, t_logits, s_logits, head, given, kept, near, lines, columns, grads, sems
):
    vocab = t_logits.shape[1]
    rows = t_logits.shape[0] // 8
    part = head.shape[0] // 4
    heads = [
        pltpu.make_async_copy(
            head.at[n * part : (n + 1) * part, :],
            near.at[n * part : (n + 1) * part, :],
            sems.at[n],
        )
        for n in range(4)
    ]
    for copy in heads:
        copy.start()
    total = joined(got, 8 * rows)
    lines[...] = jnp.zeros_like(lines)
    lines[0:1, :] = total[:, : 8 * rows]
    lines[1:2, :] = total[:, 8 * rows :]
    columns[...] = lines[...].T
    mine = own_place(ids)
    for r in range(8):
        here = slice(r * rows, (r + 1) * rows)
        logs = columns[block_rows(mine ^ r, rows), :]
        t_prob = jnp.exp(t_logits[here, :] - logs[:, 0:1])
        s_prob = jnp.exp(s_logits[here, :] - logs[:, 1:2])
        hit = labels[here, :] - ids[4] * vocab == lane(t_prob.shape)
        grad = scale[here, :] * ((1.0 + BETA) * s_prob - t_prob - BETA * hit.astype(F32))
        place = (r // 4) * 2 + r % 2
        into = grads if (r // 2) % 2 else kept
        into[place * rows : (place + 1) * rows, :] = grad.astype(BF16)
    for n, copy in enumerate(heads):
        copy.wait()
        here = slice(n * part, (n + 1) * part)
        given[:, here] = lax.dot_general(
            grads[...], near[here, :], (((1,), (1,)), ((), ())), preferred_element_type=F32
        ).astype(BF16)


def kept_kernel(ids, grads, head, out):
    product_into(out, grads, head)


def prep_kernel(live, share, nseq, ids, *refs):
    packed, (labels, scale, weights, turned) = refs[:4], refs[4:]
    tok = turned.shape[0]
    places = lane((1, tok))
    turned[...] = jnp.zeros_like(turned)
    for g, ref in enumerate(packed):
        start = jnp.zeros((1, 1), jnp.int32)
        covered = jnp.zeros((1, tok), jnp.int32)
        spans = jnp.zeros((1, tok), jnp.int32)
        for n in range(nseq):
            length = ref[:, tok + n : tok + n + 1]
            inside = ((places >= start) & (places < start + length)).astype(jnp.int32)
            covered = covered + inside
            spans = spans + inside * length
            start = start + length
        weight = covered.astype(F32) / jnp.maximum(spans, 1).astype(F32)
        if g == 0:
            weights[...] = weight
        turned[g : g + 1, :] = ref[:, :tok].astype(F32)
        turned[4 + g : 5 + g, :] = LOSS_SCALE * weight
    turned[...] = turned[...].T
    for i in range(8):
        g, d = i // 2, i % 2
        for z in range(live):
            there = slice((i * live + z) * share, (i * live + z + 1) * share)
            here = block_rows(2 * z + (ids[3] ^ d), share)
            block = turned[here, :]
            labels[there, :] = block[:, g : g + 1].astype(jnp.int32)
            scale[there, :] = block[:, 4 + g : 5 + g]


def loss_kernel(live, share, ids, got, weights, loss):
    tok = weights.shape[1]
    rows = 8 * live * share
    total = joined(got, rows)
    t_log = total[:, :rows]
    s_log = total[:, rows:]
    cross, value = 0.0, 0.0
    for d in range(got.shape[0]):
        part = got[d]
        cross = cross + jnp.exp(part[:, :rows] - t_log) * part[:, 2 * rows : 3 * rows]
        value = value + part[:, 3 * rows :]
    line = cross - t_log + s_log + BETA * (s_log - value)
    slot = jnp.minimum(ids[2], live - 1)
    at = (own_place(ids) * live + slot) * share
    own = pltpu.roll(line, rows - at, 1)[:, :128]
    weight = pltpu.roll(weights[...], tok - (2 * slot + ids[3]) * share, 1)[:, :128]
    keep = (weight > 0) & (ids[2] < live)
    loss[...] = jnp.where(keep, own, 0.0)


def add_kernel(ids, kept, other, own, to_x, to_y, to_far):
    rows = own.shape[0]
    own[...] = kept[:rows, :] + other[:rows, :].astype(F32)
    for i, out in ((1, to_x), (2, to_y), (3, to_far)):
        here = slice(i * rows, (i + 1) * rows)
        out[...] = (kept[here, :] + other[here, :].astype(F32)).astype(BF16)


def chunk_kernel(live, ids, base, by_x, by_y, far, own, *lows):
    share = own.shape[0]

    def chunk(slot):
        here = block_rows(jnp.minimum(slot, live - 1), share)
        total = base[here, :] + by_x[here, :].astype(F32)
        return total + by_y[here, :].astype(F32) + far[here, :].astype(F32)

    own[...] = chunk(ids[2])
    for k, low in enumerate(lows, 1):
        low[...] = chunk(ids[2] ^ k).astype(BF16)


def final_kernel(live, ids, own, *refs):
    chunks, (hidden, gain, out) = refs[:-3], refs[-3:]
    summed = own[...]
    for chunk in chunks:
        summed = summed + chunk[...].astype(F32)
    out[...] = hidden_gradient(summed, hidden[...].astype(F32), gain[...])

    @pl.when(ids[2] >= live)
    def _():
        out[...] = jnp.zeros_like(out)


def hidden_gradient(summed, hidden, gain):
    inverse = lax.rsqrt(jnp.mean(hidden * hidden, axis=-1, keepdims=True) + EPS)
    scaled = summed * gain
    inner = jnp.mean(scaled * hidden, axis=1, keepdims=True)
    return inverse * scaled - hidden * (inverse * inverse * inverse) * inner


def reduce_rows(grid, kept, other, share):
    rows, width = kept.shape[0] // 4, kept.shape[1]
    own, to_x, to_y, to_far = call(
        add_kernel,
        grid.ids,
        [kept, other],
        [shape_of((rows, width), F32)] + [shape_of((rows, width), BF16)] * 3,
        [],
        4,
    )
    by_x = grid.send(to_x, d=1)
    by_y = grid.send(to_y, a=1)
    far = grid.send(to_far, a=1, d=1)
    ks = range(1, grid.depth)
    if grid.tiled:
        summed, *lows = call(
            functools.partial(chunk_kernel, grid.live),
            grid.ids,
            [own, by_x, by_y, far],
            [shape_of((share, width), F32)] + [shape_of((share, width), BF16) for k in ks],
            [],
            4,
        )
    else:
        mine = own + by_x.astype(F32) + by_y.astype(F32) + far.astype(F32)
        mine = mine.reshape(grid.live, share, width)
        slots = [jnp.minimum(grid.z ^ k, grid.live - 1) for k in range(grid.depth)]
        summed, *lows = [lax.dynamic_index_in_dim(mine, k, 0, keepdims=False) for k in slots]
        lows = [low.astype(BF16) for low in lows]
    return summed, [grid.send(low, k=k, target=grid.live) for k, low in zip(ks, lows)]


def row_weights(lengths, tok_rows):
    ends = jnp.cumsum(lengths, axis=1)
    starts = ends - lengths
    places = jnp.arange(tok_rows, dtype=jnp.int32)
    inside = (places[None, :, None] >= starts[:, None, :]) & (
        places[None, :, None] < ends[:, None, :]
    )
    spans = jnp.sum(jnp.where(inside, lengths[:, None, :], 0), axis=2)
    covered = jnp.sum(inside.astype(jnp.int32), axis=2)
    return covered.astype(F32) / jnp.maximum(spans, 1).astype(F32)


def shards(
    teacher_partial,
    teacher_residual,
    post_gain,
    final_gain,
    teacher_head,
    student_hidden,
    student_gain,
    student_head,
    labels,
    lengths,
):
    share, width_t = teacher_residual.shape
    width_s = student_hidden.shape[1]
    tok_rows = labels.shape[0]
    nseq = lengths.shape[1]
    grid = Grid(lax.axis_size("dp"), lax.axis_size("tp"), share)
    live = grid.live

    parts = teacher_partial[0, :LIVE].reshape(live, 2, share, width_t)
    given = lax.dynamic_index_in_dim(parts, 1 - grid.x, 1, keepdims=False)
    other = grid.send(given, d=1)
    at = jnp.minimum(grid.z, live - 1)
    ks = range(1, grid.depth)
    if grid.tiled:
        own, *lows = call(
            functools.partial(pair_kernel, live),
            grid.ids,
            [teacher_partial, other],
            [shape_of((share, width_t), F32)] + [shape_of((share, width_t), BF16) for k in ks],
            [],
            4,
        )
    else:
        kept = lax.dynamic_index_in_dim(parts, grid.x, 1, keepdims=False)
        pair = kept.astype(F32) + other.astype(F32)
        own = lax.dynamic_index_in_dim(pair, at, 0, keepdims=False)
        lows = [
            lax.dynamic_index_in_dim(
                pair, jnp.minimum(grid.z ^ k, live - 1), 0, keepdims=False
            ).astype(BF16)
            for k in ks
        ]
    others = [grid.send(low, k=k, target=live) for k, low in zip(ks, lows)]

    student_f = student_hidden.astype(F32)
    student_norm = norm_rows(student_f, student_gain)[0].astype(BF16)
    own_s = gather_depth(grid, student_norm)
    whole_s = gather_plane(grid, own_s)

    ints = jnp.concatenate([labels, lengths[0]])[None]
    packed = [ints] + [grid.send(ints, a=a, b=b) for a, b in ((0, 1), (1, 0), (1, 1))]

    def by_row(value):
        value = value[:, :LIVE].reshape(4, live, 2, share)
        value = jnp.moveaxis(value, 2, 1)
        value = jnp.where(grid.x == 1, jnp.flip(value, 1), value)
        return value.reshape(-1)[:, None]

    rows = 8 * live * share
    if grid.tiled:
        label_column, scale_column, weight_line = call(
            functools.partial(prep_kernel, live, share, nseq),
            grid.ids,
            packed,
            [
                shape_of((rows, 1), jnp.int32),
                shape_of((rows, 1), F32),
                shape_of((1, tok_rows), F32),
            ],
            [pltpu.VMEM((tok_rows, 128), F32)],
            4,
        )
    else:
        whole = jnp.concatenate(packed, axis=0)
        weight_rows = row_weights(whole[:, tok_rows : tok_rows + nseq], tok_rows)
        label_column = by_row(whole[:, :tok_rows])
        scale_column = by_row(LOSS_SCALE * weight_rows)
        weight_line = weight_rows[:1]

    if grid.tiled:
        teacher_norm = call(
            norm_kernel,
            grid.ids,
            [own, *others, teacher_residual, post_gain[None], final_gain[None]],
            [shape_of((share, width_t), BF16)],
            [],
            4,
        )[0]
    else:
        mlp_sum = own
        for other in others:
            mlp_sum = mlp_sum + other.astype(F32)
        post, _ = norm_rows(mlp_sum, post_gain)
        final = teacher_residual.astype(F32) + post
        teacher_norm = norm_rows(final, final_gain)[0].astype(BF16)
    own_t = gather_depth(grid, teacher_norm)
    whole_t = gather_plane(grid, own_t)

    vocab_dev = student_head.shape[1]

    s_logits = jnp.dot(whole_s, student_head, preferred_element_type=F32)
    s_cols = call(
        student_kernel, grid.ids, [s_logits, label_column], [shape_of((rows, 128), F32)], [], 4
    )[0]
    t_logits = jnp.dot(whole_t, teacher_head, preferred_element_type=F32)
    devices = 4 * grid.tp
    sent = call(
        teacher_kernel,
        grid.ids,
        [t_logits, s_logits, s_cols],
        [shape_of((devices, 1, 4 * rows), F32)],
        [pltpu.VMEM((rows, 128), F32)],
        8,
    )[0]
    got = lax.all_to_all(sent, AXES, 0, 0, tiled=True)

    half = rows // 2
    given, grads, near = call(
        given_kernel,
        grid.ids,
        [got, label_column, scale_column, t_logits, s_logits],
        [
            shape_of((half, width_s), BF16),
            shape_of((half, vocab_dev), BF16),
            shape_of(student_head.shape, BF16),
        ],
        [
            pltpu.VMEM((128, rows), F32),
            pltpu.VMEM((rows, 128), F32),
            pltpu.VMEM((half, vocab_dev), BF16),
            pltpu.SemaphoreType.DMA((4,)),
        ],
        10,
        [student_head],
    )
    other = grid.send(given, b=1)
    kept = call(kept_kernel, grid.ids, [grads, near], [shape_of((half, width_s), F32)], [], 4)[0]
    summed, chunks = reduce_rows(grid, kept, other, share)
    row_loss = call(
        functools.partial(loss_kernel, live, share),
        grid.ids,
        [got, weight_line],
        [shape_of((1, 128), F32)],
        [],
        4,
    )[0]
    if grid.tiled:
        grad_hidden = call(
            functools.partial(final_kernel, live),
            grid.ids,
            [summed, *chunks, student_hidden, student_gain[None]],
            [jax.ShapeDtypeStruct((share, width_s), F32)],
            [],
            4,
        )[0]
    else:
        for chunk in chunks:
            summed = summed + chunk.astype(F32)
        grad_hidden = jnp.where(
            grid.z < live, hidden_gradient(summed, student_f, student_gain), 0.0
        )
    return (grad_hidden, row_loss[0, :share])


def solution(mesh):
    placed = (
        P("tp", "dp", None),
        P(("dp", "tp"), None),
        P(),
        P(),
        P(None, ("dp", "tp")),
        P(("dp", "tp"), None),
        P(),
        P(None, ("dp", "tp")),
        P("dp"),
        P("dp", None),
    )
    return jax.shard_map(
        shards,
        mesh=mesh,
        in_specs=placed,
        out_specs=(P(("dp", "tp"), None), P(("dp", "tp"))),
        check_vma=False,
    )
```

```python
import functools

import jax
import jax.numpy as jnp
from jax import lax
from jax.experimental import pallas as pl
from jax.experimental.pallas import tpu as pltpu
from jax.sharding import PartitionSpec as P


EPS = 1e-06
BETA = 0.5
LOSS_SCALE = 1024.0
LIVE = 96
PARTS = 2
F32 = jnp.float32
BF16 = jnp.bfloat16
AXES = ("dp", "tp")


class Grid:
    def __init__(self, dp, tp, share):
        assert dp == 4 and tp % 2 == 0
        self.tp, self.depth = tp, tp // 2
        self.live = LIVE // (2 * share)
        assert self.live * 2 * share == LIVE
        dp_at, tp_at = lax.axis_index("dp"), lax.axis_index("tp")
        self.y, self.c = dp_at // 2, dp_at % 2
        self.z, self.x = tp_at // 2, tp_at % 2
        self.tiled = share % 16 == 0
        self.ids = jnp.stack([self.y, self.c, self.z, self.x, dp_at * tp + tp_at])

    def send(self, value, a=0, b=0, k=0, d=0, source=None, target=None):
        pairs = []
        for dp_at in range(4):
            for tp_at in range(self.tp):
                z = tp_at // 2
                if source is not None and z >= source:
                    continue
                if target is not None and (z ^ k) >= target:
                    continue
                to = (dp_at ^ (2 * a + b)) * self.tp + (tp_at ^ (2 * k + d))
                pairs.append((dp_at * self.tp + tp_at, to))
        return lax.ppermute(value, AXES, pairs)

    def send_depth(self, values, source=None, target=None):
        got = []
        for k, value in enumerate(values, 1):
            got.append(self.send(value, k=k, source=source, target=target))
        return got


def pick(pieces, index):
    bit = 0
    while len(pieces) > 1:
        high = (index >> bit) & 1
        pieces = [jnp.where(high == 1, pieces[i + 1], pieces[i]) for i in range(0, len(pieces), 2)]
        bit += 1
    return pieces[0]


def norm_rows(values, gain):
    inverse = lax.rsqrt(jnp.mean(values * values, axis=-1, keepdims=True) + EPS)
    return (values * inverse * gain, inverse)


VMEM = pl.BlockSpec(memory_space=pltpu.VMEM)
SMEM = pl.BlockSpec(memory_space=pltpu.SMEM)
shape_of = pltpu.VMEM
MIB = 1 << 20


def call(kernel, ids, args, outs, scratch, mib, far=()):
    args = [pltpu.with_memory_space_constraint(arg, pltpu.VMEM) for arg in args]
    far = [pltpu.with_memory_space_constraint(arg, pltpu.HBM) for arg in far]
    return pl.pallas_call(
        kernel,
        out_shape=outs,
        in_specs=[SMEM] + [VMEM] * len(args) + [pl.BlockSpec(memory_space=pltpu.HBM)] * len(far),
        out_specs=[VMEM] * len(outs),
        scratch_shapes=scratch,
        compiler_params=pltpu.CompilerParams(vmem_limit_bytes=mib * MIB),
    )(ids, *args, *far)


def pick_kernel(live, ids, *refs):
    pieces, out = refs[:-1], refs[-1]
    share = pieces[0].shape[0]
    for j in range(live):
        for k, piece in enumerate(pieces):

            @pl.when((ids[2] ^ j) == k)
            def _(j=j, piece=piece):
                out[j * share : (j + 1) * share, :] = piece[...]


def pair_kernel(live, ids, partial, other, own, *lows):
    share = own.shape[0]

    def chunk(slot):
        slot = jnp.minimum(slot, live - 1)
        at = pl.multiple_of((2 * slot + ids[3]) * share, share)
        return partial[0, pl.ds(at, share), :].astype(F32) + other[slot].astype(F32)

    own[...] = chunk(ids[2])
    for k, low in enumerate(lows, 1):
        low[...] = chunk(ids[2] ^ k).astype(BF16)


def norm_kernel(ids, *refs):
    own, others = refs[0], refs[1:-4]
    residual, post_gain, final_gain, out = refs[-4:]
    total = own[...]
    for other in others:
        total = total + other[...].astype(F32)
    post, _ = norm_rows(total, post_gain[...])
    final = residual[...].astype(F32) + post
    out[...] = norm_rows(final, final_gain[...])[0].astype(BF16)


def gather_depth(grid, rows):
    pieces = [rows] + grid.send_depth([rows] * (grid.depth - 1), source=grid.live)
    if not grid.tiled:
        return jnp.concatenate([pick(pieces, grid.z ^ j) for j in range(grid.live)], axis=0)
    return call(
        functools.partial(pick_kernel, grid.live),
        grid.ids,
        pieces,
        [shape_of((grid.live * rows.shape[0], rows.shape[1]), rows.dtype)],
        [],
        4,
    )[0]


def gather_plane(grid, own):
    by_x = grid.send(own, d=1)
    by_y = grid.send(own, a=1)
    far = grid.send(own, a=1, d=1)
    own_c = grid.send(own, b=1)
    by_x_c = grid.send(by_x, b=1)
    by_y_c = grid.send(by_y, b=1)
    far_c = grid.send(far, b=1)
    return jnp.concatenate([own, by_x, own_c, by_x_c, by_y, far, by_y_c, far_c], axis=0)


def lane(shape):
    return lax.broadcasted_iota(jnp.int32, shape, 1)


def own_place(ids):
    return ids[0] * 4 + ids[1] * 2 + ids[3]


def block_rows(number, rows):
    return pl.ds(pl.multiple_of(number * rows, rows), rows)


def student_kernel(ids, logits, labels, cols):
    vocab = logits.shape[1]
    rows = logits.shape[0] // 8
    mine = own_place(ids)

    def step(r, carry):
        here = block_rows(r, rows)
        block = logits[here, :]
        top = jnp.max(block, axis=1, keepdims=True)
        log = top + jnp.log(jnp.sum(jnp.exp(block - top), axis=1, keepdims=True))
        hit = labels[here, :] - ids[4] * vocab == lane(block.shape)
        value = jnp.sum(jnp.where(hit, block, 0.0), axis=1, keepdims=True)
        places = lane((rows, 128))
        cols[block_rows(mine ^ r, rows), :] = jnp.where(
            places == 1, log, jnp.where(places == 3, value, 0.0)
        )
        return carry

    lax.fori_loop(0, 8, step, 0)


def teacher_kernel(ids, logits, s_logits, s_cols, sent, cols):
    rows = logits.shape[0] // 8
    mine = own_place(ids)

    def step(r, carry):
        here = block_rows(r, rows)
        block = logits[here, :]
        top = jnp.max(block, axis=1, keepdims=True)
        weights = jnp.exp(block - top)
        total = jnp.sum(weights, axis=1, keepdims=True)
        mix = jnp.sum(weights * (block - s_logits[here, :]), axis=1, keepdims=True) / total
        places = lane((rows, 128))
        log = top + jnp.log(total)
        there = block_rows(mine ^ r, rows)
        cols[there, :] = jnp.where(
            places == 0, log, jnp.where(places == 2, mix, s_cols[there, :])
        )
        return carry

    lax.fori_loop(0, 8, step, 0, unroll=4)
    turned = cols[...].T
    message = jnp.concatenate([turned[n : n + 1, :] for n in range(4)], axis=1)
    for d in range(sent.shape[0]):
        sent[d] = message


def joined(got, rows):
    every = [got[d][:, : 2 * rows] for d in range(got.shape[0])]
    top = functools.reduce(jnp.maximum, every)
    return top + jnp.log(sum([jnp.exp(part - top) for part in every[1:]], jnp.exp(every[0] - top)))


def product_kernel(part, ids, grads, head, out):
    height = out.shape[1] // 2
    for n in range(2):
        here = slice(part * out.shape[1] + n * height, part * out.shape[1] + (n + 1) * height)
        value = lax.dot_general(
            grads[...], head[here, :], (((1,), (1,)), ((), ())), preferred_element_type=F32
        )
        out[:, n * height : (n + 1) * height] = value.astype(out.dtype)


def given_kernel(
    ids, got, labels, scale, t_logits, s_logits, head, given, kept, grads, near, lines, columns, sems
):
    vocab = t_logits.shape[1]
    rows = t_logits.shape[0] // 8
    part = head.shape[0] // 4
    heads = [
        pltpu.make_async_copy(
            head.at[n * part : (n + 1) * part, :],
            near.at[n * part : (n + 1) * part, :],
            sems.at[n],
        )
        for n in range(4)
    ]
    for copy in heads:
        copy.start()
    total = joined(got, 8 * rows)
    lines[...] = jnp.zeros_like(lines)
    lines[0:1, :] = total[:, : 8 * rows]
    lines[1:2, :] = total[:, 8 * rows :]
    columns[...] = lines[...].T
    mine = own_place(ids)
    for r in range(8):
        here = slice(r * rows, (r + 1) * rows)
        logs = columns[block_rows(mine ^ r, rows), :]
        t_prob = jnp.exp(t_logits[here, :] - logs[:, 0:1])
        s_prob = jnp.exp(s_logits[here, :] - logs[:, 1:2])
        hit = labels[here, :] - ids[4] * vocab == lane(t_prob.shape)
        grad = scale[here, :] * ((1.0 + BETA) * s_prob - t_prob - BETA * hit.astype(F32))
        place = (r // 4) * 2 + r % 2
        into = grads if (r // 2) % 2 else kept
        into[place * rows : (place + 1) * rows, :] = grad.astype(BF16)
    for n, copy in enumerate(heads):
        copy.wait()
        if n < 4 // PARTS:
            here = slice(n * part, (n + 1) * part)
            given[:, here] = lax.dot_general(
                grads[...], near[here, :], (((1,), (1,)), ((), ())), preferred_element_type=F32
            ).astype(BF16)


def prep_kernel(live, share, nseq, ids, *refs):
    packed, (labels, scale, weights, turned) = refs[:4], refs[4:]
    tok = turned.shape[0]
    places = lane((1, tok))
    turned[...] = jnp.zeros_like(turned)
    for g, ref in enumerate(packed):
        start = jnp.zeros((1, 1), jnp.int32)
        covered = jnp.zeros((1, tok), jnp.int32)
        spans = jnp.zeros((1, tok), jnp.int32)
        for n in range(nseq):
            length = ref[:, tok + n : tok + n + 1]
            inside = ((places >= start) & (places < start + length)).astype(jnp.int32)
            covered = covered + inside
            spans = spans + inside * length
            start = start + length
        weight = covered.astype(F32) / jnp.maximum(spans, 1).astype(F32)
        if g == 0:
            weights[...] = weight
        turned[g : g + 1, :] = ref[:, :tok].astype(F32)
        turned[4 + g : 5 + g, :] = LOSS_SCALE * weight
    turned[...] = turned[...].T
    for i in range(8):
        g, d = i // 2, i % 2
        for z in range(live):
            there = slice((i * live + z) * share, (i * live + z + 1) * share)
            here = block_rows(2 * z + (ids[3] ^ d), share)
            block = turned[here, :]
            labels[there, :] = block[:, g : g + 1].astype(jnp.int32)
            scale[there, :] = block[:, 4 + g : 5 + g]


def loss_kernel(live, share, ids, got, weights, loss):
    tok = weights.shape[1]
    rows = 8 * live * share
    total = joined(got, rows)
    t_log = total[:, :rows]
    s_log = total[:, rows:]
    cross, value = 0.0, 0.0
    for d in range(got.shape[0]):
        part = got[d]
        cross = cross + jnp.exp(part[:, :rows] - t_log) * part[:, 2 * rows : 3 * rows]
        value = value + part[:, 3 * rows :]
    line = cross - t_log + s_log + BETA * (s_log - value)
    slot = jnp.minimum(ids[2], live - 1)
    at = (own_place(ids) * live + slot) * share
    own = pltpu.roll(line, rows - at, 1)[:, :128]
    weight = pltpu.roll(weights[...], tok - (2 * slot + ids[3]) * share, 1)[:, :128]
    keep = (weight > 0) & (ids[2] < live)
    loss[...] = jnp.where(keep, own, 0.0)


def add_kernel(ids, kept, other, own, *outs):
    rows = own.shape[0]
    own[...] = kept[:rows, :] + other[:rows, :].astype(F32)
    for i, out in enumerate(outs, 1):
        here = slice(i * rows, (i + 1) * rows)
        out[...] = (kept[here, :] + other[here, :].astype(F32)).astype(BF16)


def chunk_kernel(live, ids, *refs):
    parts, (own, *lows) = refs[: 4 * PARTS], refs[4 * PARTS :]
    share, width = own.shape[0], own.shape[1] // PARTS

    def chunk(out, slot):
        here = block_rows(jnp.minimum(slot, live - 1), share)
        for part in range(PARTS):
            base, by_x, by_y, far = parts[4 * part : 4 * part + 4]
            total = base[here, :] + by_x[here, :].astype(F32)
            total = total + by_y[here, :].astype(F32) + far[here, :].astype(F32)
            out[:, part * width : (part + 1) * width] = total.astype(out.dtype)

    chunk(own, ids[2])
    for k, low in enumerate(lows, 1):
        chunk(low, ids[2] ^ k)


def final_kernel(live, ids, own, *refs):
    chunks, (hidden, gain, out) = refs[:-3], refs[-3:]
    summed = own[...]
    for chunk in chunks:
        summed = summed + chunk[...].astype(F32)
    out[...] = hidden_gradient(summed, hidden[...].astype(F32), gain[...])

    @pl.when(ids[2] >= live)
    def _():
        out[...] = jnp.zeros_like(out)


def hidden_gradient(summed, hidden, gain):
    inverse = lax.rsqrt(jnp.mean(hidden * hidden, axis=-1, keepdims=True) + EPS)
    scaled = summed * gain
    inner = jnp.mean(scaled * hidden, axis=1, keepdims=True)
    return inverse * scaled - hidden * (inverse * inverse * inverse) * inner


def product(grid, grads, head, part, dtype):
    return call(
        functools.partial(product_kernel, part),
        grid.ids,
        [grads, head],
        [shape_of((grads.shape[0], head.shape[0] // PARTS), dtype)],
        [],
        6,
    )[0]


def reduce_plane(grid, kept, other):
    rows, width = kept.shape[0] // 4, kept.shape[1]
    own, to_x, to_y, to_far = call(
        add_kernel,
        grid.ids,
        [kept, other],
        [shape_of((rows, width), F32)] + [shape_of((rows, width), BF16)] * 3,
        [],
        4,
    )
    return own, grid.send(to_x, d=1), grid.send(to_y, a=1), grid.send(to_far, a=1, d=1)


def reduce_depth(grid, parts, share):
    width = PARTS * parts[0][0].shape[1]
    if grid.tiled:
        summed, *lows = call(
            functools.partial(chunk_kernel, grid.live),
            grid.ids,
            [value for part in parts for value in part],
            [shape_of((share, width), F32)] + [shape_of((share, width), BF16)] * (grid.depth - 1),
            [],
            4,
        )
    else:
        mine = jnp.concatenate([sum([value.astype(F32) for value in part]) for part in parts], axis=1)
        mine = mine.reshape(grid.live, share, width)
        slots = [jnp.minimum(grid.z ^ k, grid.live - 1) for k in range(grid.depth)]
        summed, *lows = [lax.dynamic_index_in_dim(mine, k, 0, keepdims=False) for k in slots]
        lows = [low.astype(BF16) for low in lows]
    return [summed] + grid.send_depth(lows, target=grid.live)


def row_weights(lengths, tok_rows):
    ends = jnp.cumsum(lengths, axis=1)
    starts = ends - lengths
    places = jnp.arange(tok_rows, dtype=jnp.int32)
    inside = (places[None, :, None] >= starts[:, None, :]) & (
        places[None, :, None] < ends[:, None, :]
    )
    spans = jnp.sum(jnp.where(inside, lengths[:, None, :], 0), axis=2)
    covered = jnp.sum(inside.astype(jnp.int32), axis=2)
    return covered.astype(F32) / jnp.maximum(spans, 1).astype(F32)


def shards(
    teacher_partial,
    teacher_residual,
    post_gain,
    final_gain,
    teacher_head,
    student_hidden,
    student_gain,
    student_head,
    labels,
    lengths,
):
    share, width_t = teacher_residual.shape
    width_s = student_hidden.shape[1]
    tok_rows = labels.shape[0]
    nseq = lengths.shape[1]
    grid = Grid(lax.axis_size("dp"), lax.axis_size("tp"), share)
    live = grid.live

    parts = teacher_partial[0, :LIVE].reshape(live, 2, share, width_t)
    given = lax.dynamic_index_in_dim(parts, 1 - grid.x, 1, keepdims=False)
    other = grid.send(given, d=1)
    at = jnp.minimum(grid.z, live - 1)
    ks = range(1, grid.depth)
    if grid.tiled:
        own, *lows = call(
            functools.partial(pair_kernel, live),
            grid.ids,
            [teacher_partial, other],
            [shape_of((share, width_t), F32)] + [shape_of((share, width_t), BF16) for k in ks],
            [],
            4,
        )
    else:
        kept = lax.dynamic_index_in_dim(parts, grid.x, 1, keepdims=False)
        pair = kept.astype(F32) + other.astype(F32)
        own = lax.dynamic_index_in_dim(pair, at, 0, keepdims=False)
        lows = [
            lax.dynamic_index_in_dim(
                pair, jnp.minimum(grid.z ^ k, live - 1), 0, keepdims=False
            ).astype(BF16)
            for k in ks
        ]
    others = grid.send_depth(lows, target=live)

    student_f = student_hidden.astype(F32)
    student_norm = norm_rows(student_f, student_gain)[0].astype(BF16)
    own_s = gather_depth(grid, student_norm)
    whole_s = gather_plane(grid, own_s)

    ints = jnp.concatenate([labels, lengths[0]])[None]
    packed = [ints] + [grid.send(ints, a=a, b=b) for a, b in ((0, 1), (1, 0), (1, 1))]

    def by_row(value):
        value = value[:, :LIVE].reshape(4, live, 2, share)
        value = jnp.moveaxis(value, 2, 1)
        value = jnp.where(grid.x == 1, jnp.flip(value, 1), value)
        return value.reshape(-1)[:, None]

    rows = 8 * live * share
    if grid.tiled:
        label_column, scale_column, weight_line = call(
            functools.partial(prep_kernel, live, share, nseq),
            grid.ids,
            packed,
            [
                shape_of((rows, 1), jnp.int32),
                shape_of((rows, 1), F32),
                shape_of((1, tok_rows), F32),
            ],
            [pltpu.VMEM((tok_rows, 128), F32)],
            4,
        )
    else:
        whole = jnp.concatenate(packed, axis=0)
        weight_rows = row_weights(whole[:, tok_rows : tok_rows + nseq], tok_rows)
        label_column = by_row(whole[:, :tok_rows])
        scale_column = by_row(LOSS_SCALE * weight_rows)
        weight_line = weight_rows[:1]

    if grid.tiled:
        teacher_norm = call(
            norm_kernel,
            grid.ids,
            [own, *others, teacher_residual, post_gain[None], final_gain[None]],
            [shape_of((share, width_t), BF16)],
            [],
            4,
        )[0]
    else:
        mlp_sum = own
        for other in others:
            mlp_sum = mlp_sum + other.astype(F32)
        post, _ = norm_rows(mlp_sum, post_gain)
        final = teacher_residual.astype(F32) + post
        teacher_norm = norm_rows(final, final_gain)[0].astype(BF16)
    own_t = gather_depth(grid, teacher_norm)
    whole_t = gather_plane(grid, own_t)

    vocab_dev = student_head.shape[1]

    s_logits = jnp.dot(whole_s, student_head, preferred_element_type=F32)
    s_cols = call(
        student_kernel, grid.ids, [s_logits, label_column], [shape_of((rows, 128), F32)], [], 4
    )[0]
    t_logits = jnp.dot(whole_t, teacher_head, preferred_element_type=F32)
    devices = 4 * grid.tp
    sent = call(
        teacher_kernel,
        grid.ids,
        [t_logits, s_logits, s_cols],
        [shape_of((devices, 1, 4 * rows), F32)],
        [pltpu.VMEM((rows, 128), F32)],
        8,
    )[0]
    got = lax.all_to_all(sent, AXES, 0, 0, tiled=True)

    half = rows // 2
    given, keeps, gives, near = call(
        given_kernel,
        grid.ids,
        [got, label_column, scale_column, t_logits, s_logits],
        [
            shape_of((half, width_s // PARTS), BF16),
            shape_of((half, vocab_dev), BF16),
            shape_of((half, vocab_dev), BF16),
            shape_of(student_head.shape, BF16),
        ],
        [pltpu.VMEM((128, rows), F32), pltpu.VMEM((rows, 128), F32), pltpu.SemaphoreType.DMA((4,))],
        10,
        [student_head],
    )
    others = []
    for part in range(PARTS):
        if part:
            given = product(grid, gives, near, part, BF16)
        others.append(grid.send(given, b=1))
    parts = []
    for part in range(PARTS):
        kept = product(grid, keeps, near, part, F32)
        parts.append(reduce_plane(grid, kept, others[part]))
    sums = reduce_depth(grid, parts, share)
    row_loss = call(
        functools.partial(loss_kernel, live, share),
        grid.ids,
        [got, weight_line],
        [shape_of((1, 128), F32)],
        [],
        4,
    )[0]
    if grid.tiled:
        grad_hidden = call(
            functools.partial(final_kernel, live),
            grid.ids,
            [*sums, student_hidden, student_gain[None]],
            [jax.ShapeDtypeStruct((share, width_s), F32)],
            [],
            4,
        )[0]
    else:
        summed = sum([value.astype(F32) for value in sums])
        grad_hidden = jnp.where(
            grid.z < live, hidden_gradient(summed, student_f, student_gain), 0.0
        )
    return (grad_hidden, row_loss[0, :share])


def solution(mesh):
    placed = (
        P("tp", "dp", None),
        P(("dp", "tp"), None),
        P(),
        P(),
        P(None, ("dp", "tp")),
        P(("dp", "tp"), None),
        P(),
        P(None, ("dp", "tp")),
        P("dp"),
        P("dp", None),
    )
    return jax.shard_map(
        shards,
        mesh=mesh,
        in_specs=placed,
        out_specs=(P(("dp", "tp"), None), P(("dp", "tp"))),
        check_vma=False,
    )
```

```python
import functools

import jax
import jax.numpy as jnp
from jax import lax
from jax.experimental import pallas as pl
from jax.experimental.pallas import tpu as pltpu
from jax.sharding import PartitionSpec as P


EPS = 1e-06
BETA = 0.5
LOSS_SCALE = 1024.0
LIVE = 96
PARTS = 2
F32 = jnp.float32
BF16 = jnp.bfloat16
AXES = ("dp", "tp")


class Grid:
    def __init__(self, dp, tp, share):
        assert dp == 4 and tp % 2 == 0
        self.tp, self.depth = tp, tp // 2
        self.live = LIVE // (2 * share)
        assert self.live * 2 * share == LIVE
        dp_at, tp_at = lax.axis_index("dp"), lax.axis_index("tp")
        self.y, self.c = dp_at // 2, dp_at % 2
        self.z, self.x = tp_at // 2, tp_at % 2
        self.tiled = share % 16 == 0
        self.ids = jnp.stack([self.y, self.c, self.z, self.x, dp_at * tp + tp_at])

    def send(self, value, a=0, b=0, k=0, d=0, source=None, target=None):
        pairs = []
        for dp_at in range(4):
            for tp_at in range(self.tp):
                z = tp_at // 2
                if source is not None and z >= source:
                    continue
                if target is not None and (z ^ k) >= target:
                    continue
                to = (dp_at ^ (2 * a + b)) * self.tp + (tp_at ^ (2 * k + d))
                pairs.append((dp_at * self.tp + tp_at, to))
        return lax.ppermute(value, AXES, pairs)

    def send_depth(self, values, source=None, target=None):
        got = []
        for k, value in enumerate(values, 1):
            got.append(self.send(value, k=k, source=source, target=target))
        return got


def pick(pieces, index):
    bit = 0
    while len(pieces) > 1:
        high = (index >> bit) & 1
        pieces = [jnp.where(high == 1, pieces[i + 1], pieces[i]) for i in range(0, len(pieces), 2)]
        bit += 1
    return pieces[0]


def norm_rows(values, gain):
    inverse = lax.rsqrt(jnp.mean(values * values, axis=-1, keepdims=True) + EPS)
    return (values * inverse * gain, inverse)


VMEM = pl.BlockSpec(memory_space=pltpu.VMEM)
SMEM = pl.BlockSpec(memory_space=pltpu.SMEM)
shape_of = pltpu.VMEM
MIB = 1 << 20


def call(kernel, ids, args, outs, scratch, mib, far=()):
    args = [pltpu.with_memory_space_constraint(arg, pltpu.VMEM) for arg in args]
    far = [pltpu.with_memory_space_constraint(arg, pltpu.HBM) for arg in far]
    return pl.pallas_call(
        kernel,
        out_shape=outs,
        in_specs=[SMEM] + [VMEM] * len(args) + [pl.BlockSpec(memory_space=pltpu.HBM)] * len(far),
        out_specs=[VMEM] * len(outs),
        scratch_shapes=scratch,
        compiler_params=pltpu.CompilerParams(vmem_limit_bytes=mib * MIB),
    )(ids, *args, *far)


def pick_kernel(live, ids, *refs):
    pieces, out = refs[:-1], refs[-1]
    share = pieces[0].shape[0]
    for j in range(live):
        for k, piece in enumerate(pieces):

            @pl.when((ids[2] ^ j) == k)
            def _(j=j, piece=piece):
                out[j * share : (j + 1) * share, :] = piece[...]


def pair_kernel(live, ids, kept, other, own, *lows):
    def chunk(slot):
        slot = jnp.minimum(slot, live - 1)
        return kept[slot].astype(F32) + other[slot].astype(F32)

    own[...] = chunk(ids[2])
    for k, low in enumerate(lows, 1):
        low[...] = chunk(ids[2] ^ k).astype(BF16)


def norm_kernel(ids, *refs):
    own, others = refs[0], refs[1:-4]
    residual, post_gain, final_gain, out = refs[-4:]
    total = own[...]
    for other in others:
        total = total + other[...].astype(F32)
    post, _ = norm_rows(total, post_gain[...])
    final = residual[...].astype(F32) + post
    out[...] = norm_rows(final, final_gain[...])[0].astype(BF16)


def gather_depth(grid, rows):
    pieces = [rows] + grid.send_depth([rows] * (grid.depth - 1), source=grid.live)
    if not grid.tiled:
        return jnp.concatenate([pick(pieces, grid.z ^ j) for j in range(grid.live)], axis=0)
    return call(
        functools.partial(pick_kernel, grid.live),
        grid.ids,
        pieces,
        [shape_of((grid.live * rows.shape[0], rows.shape[1]), rows.dtype)],
        [],
        4,
    )[0]


def gather_plane(grid, own):
    by_x = grid.send(own, d=1)
    by_y = grid.send(own, a=1)
    far = grid.send(own, a=1, d=1)
    own_c = grid.send(own, b=1)
    by_x_c = grid.send(by_x, b=1)
    by_y_c = grid.send(by_y, b=1)
    far_c = grid.send(far, b=1)
    return jnp.concatenate([own, by_x, own_c, by_x_c, by_y, far, by_y_c, far_c], axis=0)


def lane(shape):
    return lax.broadcasted_iota(jnp.int32, shape, 1)


def own_place(ids):
    return ids[0] * 4 + ids[1] * 2 + ids[3]


def block_rows(number, rows):
    return pl.ds(pl.multiple_of(number * rows, rows), rows)


def student_kernel(ids, logits, labels, cols):
    vocab = logits.shape[1]
    rows = logits.shape[0] // 8
    mine = own_place(ids)

    def step(r, carry):
        here = block_rows(r, rows)
        block = logits[here, :]
        top = jnp.max(block, axis=1, keepdims=True)
        log = top + jnp.log(jnp.sum(jnp.exp(block - top), axis=1, keepdims=True))
        hit = labels[here, :] - ids[4] * vocab == lane(block.shape)
        value = jnp.sum(jnp.where(hit, block, 0.0), axis=1, keepdims=True)
        places = lane((rows, 128))
        cols[block_rows(mine ^ r, rows), :] = jnp.where(
            places == 1, log, jnp.where(places == 3, value, 0.0)
        )
        return carry

    lax.fori_loop(0, 8, step, 0)


def teacher_kernel(ids, logits, s_logits, s_cols, sent, cols):
    rows = logits.shape[0] // 8
    mine = own_place(ids)

    def step(r, carry):
        here = block_rows(r, rows)
        block = logits[here, :]
        top = jnp.max(block, axis=1, keepdims=True)
        weights = jnp.exp(block - top)
        total = jnp.sum(weights, axis=1, keepdims=True)
        mix = jnp.sum(weights * (block - s_logits[here, :]), axis=1, keepdims=True) / total
        places = lane((rows, 128))
        log = top + jnp.log(total)
        there = block_rows(mine ^ r, rows)
        cols[there, :] = jnp.where(
            places == 0, log, jnp.where(places == 2, mix, s_cols[there, :])
        )
        return carry

    lax.fori_loop(0, 8, step, 0, unroll=4)
    turned = cols[...].T
    message = jnp.concatenate([turned[n : n + 1, :] for n in range(4)], axis=1)
    for d in range(sent.shape[0]):
        sent[d] = message


def joined(got, rows):
    every = [got[d][:, : 2 * rows] for d in range(got.shape[0])]
    top = functools.reduce(jnp.maximum, every)
    return top + jnp.log(sum([jnp.exp(part - top) for part in every[1:]], jnp.exp(every[0] - top)))


def logit_kernel(
    ids, got, labels, scale, t_logits, s_logits, kept, grads, lines, columns
):
    vocab = t_logits.shape[1]
    rows = t_logits.shape[0] // 8
    total = joined(got, 8 * rows)
    lines[...] = jnp.zeros_like(lines)
    lines[0:1, :] = total[:, : 8 * rows]
    lines[1:2, :] = total[:, 8 * rows :]
    columns[...] = lines[...].T
    mine = own_place(ids)
    for r in range(8):
        here = slice(r * rows, (r + 1) * rows)
        logs = columns[block_rows(mine ^ r, rows), :]
        t_prob = jnp.exp(t_logits[here, :] - logs[:, 0:1])
        s_prob = jnp.exp(s_logits[here, :] - logs[:, 1:2])
        hit = labels[here, :] - ids[4] * vocab == lane(t_prob.shape)
        grad = scale[here, :] * ((1.0 + BETA) * s_prob - t_prob - BETA * hit.astype(F32))
        place = (r // 4) * 2 + r % 2
        into = grads if (r // 2) % 2 else kept
        into[place * rows : (place + 1) * rows, :] = grad.astype(BF16)


def prep_kernel(live, share, nseq, ids, *refs):
    packed, (labels, scale, weights, turned) = refs[:4], refs[4:]
    tok = turned.shape[0]
    places = lane((1, tok))
    turned[...] = jnp.zeros_like(turned)
    for g, ref in enumerate(packed):
        start = jnp.zeros((1, 1), jnp.int32)
        covered = jnp.zeros((1, tok), jnp.int32)
        spans = jnp.zeros((1, tok), jnp.int32)
        for n in range(nseq):
            length = ref[:, tok + n : tok + n + 1]
            inside = ((places >= start) & (places < start + length)).astype(jnp.int32)
            covered = covered + inside
            spans = spans + inside * length
            start = start + length
        weight = covered.astype(F32) / jnp.maximum(spans, 1).astype(F32)
        if g == 0:
            weights[...] = weight
        turned[g : g + 1, :] = ref[:, :tok].astype(F32)
        turned[4 + g : 5 + g, :] = LOSS_SCALE * weight
    turned[...] = turned[...].T
    for i in range(8):
        g, d = i // 2, i % 2
        for z in range(live):
            there = slice((i * live + z) * share, (i * live + z + 1) * share)
            here = block_rows(2 * z + (ids[3] ^ d), share)
            block = turned[here, :]
            labels[there, :] = block[:, g : g + 1].astype(jnp.int32)
            scale[there, :] = block[:, 4 + g : 5 + g]


def loss_kernel(live, share, ids, got, weights, loss):
    tok = weights.shape[1]
    rows = 8 * live * share
    total = joined(got, rows)
    t_log = total[:, :rows]
    s_log = total[:, rows:]
    cross, value = 0.0, 0.0
    for d in range(got.shape[0]):
        part = got[d]
        cross = cross + jnp.exp(part[:, :rows] - t_log) * part[:, 2 * rows : 3 * rows]
        value = value + part[:, 3 * rows :]
    line = cross - t_log + s_log + BETA * (s_log - value)
    slot = jnp.minimum(ids[2], live - 1)
    at = (own_place(ids) * live + slot) * share
    own = pltpu.roll(line, rows - at, 1)[:, :128]
    weight = pltpu.roll(weights[...], tok - (2 * slot + ids[3]) * share, 1)[:, :128]
    keep = (weight > 0) & (ids[2] < live)
    loss[...] = jnp.where(keep, own, 0.0)


def add_kernel(ids, kept, other, own, *outs):
    rows = own.shape[0]
    own[...] = kept[:rows, :] + other[:rows, :].astype(F32)
    for i, out in enumerate(outs, 1):
        here = slice(i * rows, (i + 1) * rows)
        out[...] = (kept[here, :] + other[here, :].astype(F32)).astype(BF16)


def chunk_kernel(live, ids, *refs):
    parts, (own, *lows) = refs[: 4 * PARTS], refs[4 * PARTS :]
    share, width = own.shape[0], own.shape[1] // PARTS

    def chunk(out, slot):
        here = block_rows(jnp.minimum(slot, live - 1), share)
        for part in range(PARTS):
            base, by_x, by_y, far = parts[4 * part : 4 * part + 4]
            total = base[here, :] + by_x[here, :].astype(F32)
            total = total + by_y[here, :].astype(F32) + far[here, :].astype(F32)
            out[:, part * width : (part + 1) * width] = total.astype(out.dtype)

    chunk(own, ids[2])
    for k, low in enumerate(lows, 1):
        chunk(low, ids[2] ^ k)


def final_kernel(live, ids, own, *refs):
    chunks, (hidden, gain, out) = refs[:-3], refs[-3:]
    summed = own[...]
    for chunk in chunks:
        summed = summed + chunk[...].astype(F32)
    out[...] = hidden_gradient(summed, hidden[...].astype(F32), gain[...])

    @pl.when(ids[2] >= live)
    def _():
        out[...] = jnp.zeros_like(out)


def hidden_gradient(summed, hidden, gain):
    inverse = lax.rsqrt(jnp.mean(hidden * hidden, axis=-1, keepdims=True) + EPS)
    scaled = summed * gain
    inner = jnp.mean(scaled * hidden, axis=1, keepdims=True)
    return inverse * scaled - hidden * (inverse * inverse * inverse) * inner


def product(grads, head, part, dtype):
    width = head.shape[0] // PARTS
    return lax.dot_general(
        grads,
        head[part * width : (part + 1) * width],
        (((1,), (1,)), ((), ())),
        preferred_element_type=F32,
    ).astype(dtype)


def reduce_plane(grid, kept, other):
    rows, width = kept.shape[0] // 4, kept.shape[1]
    own, to_x, to_y, to_far = call(
        add_kernel,
        grid.ids,
        [kept, other],
        [shape_of((rows, width), F32)] + [shape_of((rows, width), BF16)] * 3,
        [],
        4,
    )
    return own, grid.send(to_x, d=1), grid.send(to_y, a=1), grid.send(to_far, a=1, d=1)


def reduce_depth(grid, parts, share):
    width = PARTS * parts[0][0].shape[1]
    if grid.tiled:
        summed, *lows = call(
            functools.partial(chunk_kernel, grid.live),
            grid.ids,
            [value for part in parts for value in part],
            [shape_of((share, width), F32)] + [shape_of((share, width), BF16)] * (grid.depth - 1),
            [],
            4,
        )
    else:
        mine = jnp.concatenate([sum([value.astype(F32) for value in part]) for part in parts], axis=1)
        mine = mine.reshape(grid.live, share, width)
        slots = [jnp.minimum(grid.z ^ k, grid.live - 1) for k in range(grid.depth)]
        summed, *lows = [lax.dynamic_index_in_dim(mine, k, 0, keepdims=False) for k in slots]
        lows = [low.astype(BF16) for low in lows]
    return [summed] + grid.send_depth(lows, target=grid.live)


def row_weights(lengths, tok_rows):
    ends = jnp.cumsum(lengths, axis=1)
    starts = ends - lengths
    places = jnp.arange(tok_rows, dtype=jnp.int32)
    inside = (places[None, :, None] >= starts[:, None, :]) & (
        places[None, :, None] < ends[:, None, :]
    )
    spans = jnp.sum(jnp.where(inside, lengths[:, None, :], 0), axis=2)
    covered = jnp.sum(inside.astype(jnp.int32), axis=2)
    return covered.astype(F32) / jnp.maximum(spans, 1).astype(F32)


def shards(
    teacher_partial,
    teacher_residual,
    post_gain,
    final_gain,
    teacher_head,
    student_hidden,
    student_gain,
    student_head,
    labels,
    lengths,
):
    share, width_t = teacher_residual.shape
    width_s = student_hidden.shape[1]
    tok_rows = labels.shape[0]
    nseq = lengths.shape[1]
    grid = Grid(lax.axis_size("dp"), lax.axis_size("tp"), share)
    live = grid.live

    zero = jnp.zeros((), jnp.int32)
    parts = teacher_partial.reshape(-1, 2, share, width_t)

    def half_of(x):
        begin = (zero, x, zero, zero)
        rows = lax.dynamic_slice(parts, begin, (live, 1, share, width_t))
        return rows.reshape(live, share, width_t)

    given = half_of(1 - grid.x)
    kept = half_of(grid.x)
    other = grid.send(given, d=1)
    at = jnp.minimum(grid.z, live - 1)
    ks = range(1, grid.depth)
    if grid.tiled:
        own, *lows = call(
            functools.partial(pair_kernel, live),
            grid.ids,
            [kept, other],
            [shape_of((share, width_t), F32)] + [shape_of((share, width_t), BF16) for k in ks],
            [],
            4,
        )
    else:
        pair = kept.astype(F32) + other.astype(F32)
        own = lax.dynamic_index_in_dim(pair, at, 0, keepdims=False)
        lows = [
            lax.dynamic_index_in_dim(
                pair, jnp.minimum(grid.z ^ k, live - 1), 0, keepdims=False
            ).astype(BF16)
            for k in ks
        ]
    others = grid.send_depth(lows, target=live)

    student_f = student_hidden.astype(F32)
    student_norm = norm_rows(student_f, student_gain)[0].astype(BF16)
    own_s = gather_depth(grid, student_norm)
    whole_s = gather_plane(grid, own_s)

    ints = jnp.concatenate([labels, lengths[0]])[None]
    packed = [ints] + [grid.send(ints, a=a, b=b) for a, b in ((0, 1), (1, 0), (1, 1))]

    def by_row(value):
        value = value[:, :LIVE].reshape(4, live, 2, share)
        value = jnp.moveaxis(value, 2, 1)
        value = jnp.where(grid.x == 1, jnp.flip(value, 1), value)
        return value.reshape(-1)[:, None]

    rows = 8 * live * share
    if grid.tiled:
        label_column, scale_column, weight_line = call(
            functools.partial(prep_kernel, live, share, nseq),
            grid.ids,
            packed,
            [
                shape_of((rows, 1), jnp.int32),
                shape_of((rows, 1), F32),
                shape_of((1, tok_rows), F32),
            ],
            [pltpu.VMEM((tok_rows, 128), F32)],
            4,
        )
    else:
        whole = jnp.concatenate(packed, axis=0)
        weight_rows = row_weights(whole[:, tok_rows : tok_rows + nseq], tok_rows)
        label_column = by_row(whole[:, :tok_rows])
        scale_column = by_row(LOSS_SCALE * weight_rows)
        weight_line = weight_rows[:1]

    if grid.tiled:
        teacher_norm = call(
            norm_kernel,
            grid.ids,
            [own, *others, teacher_residual, post_gain[None], final_gain[None]],
            [shape_of((share, width_t), BF16)],
            [],
            4,
        )[0]
    else:
        mlp_sum = own
        for other in others:
            mlp_sum = mlp_sum + other.astype(F32)
        post, _ = norm_rows(mlp_sum, post_gain)
        final = teacher_residual.astype(F32) + post
        teacher_norm = norm_rows(final, final_gain)[0].astype(BF16)
    own_t = gather_depth(grid, teacher_norm)
    whole_t = gather_plane(grid, own_t)

    vocab_dev = student_head.shape[1]

    s_logits = jnp.dot(whole_s, student_head, preferred_element_type=F32)
    s_cols = call(
        student_kernel, grid.ids, [s_logits, label_column], [shape_of((rows, 128), F32)], [], 4
    )[0]
    t_logits = jnp.dot(whole_t, teacher_head, preferred_element_type=F32)
    devices = 4 * grid.tp
    sent = call(
        teacher_kernel,
        grid.ids,
        [t_logits, s_logits, s_cols],
        [shape_of((devices, 1, 4 * rows), F32)],
        [pltpu.VMEM((rows, 128), F32)],
        8,
    )[0]
    got = lax.all_to_all(sent, AXES, 0, 0, tiled=True)

    half = rows // 2
    keeps, gives = call(
        logit_kernel,
        grid.ids,
        [got, label_column, scale_column, t_logits, s_logits],
        [shape_of((half, vocab_dev), BF16), shape_of((half, vocab_dev), BF16)],
        [pltpu.VMEM((128, rows), F32), pltpu.VMEM((rows, 128), F32)],
        6,
    )
    others = []
    for part in range(PARTS):
        given = product(gives, student_head, part, BF16)
        others.append(grid.send(given, b=1))
    parts = []
    for part in range(PARTS):
        kept = product(keeps, student_head, part, F32)
        parts.append(reduce_plane(grid, kept, others[part]))
    sums = reduce_depth(grid, parts, share)
    row_loss = call(
        functools.partial(loss_kernel, live, share),
        grid.ids,
        [got, weight_line],
        [shape_of((1, 128), F32)],
        [],
        4,
    )[0]
    if grid.tiled:
        grad_hidden = call(
            functools.partial(final_kernel, live),
            grid.ids,
            [*sums, student_hidden, student_gain[None]],
            [jax.ShapeDtypeStruct((share, width_s), F32)],
            [],
            4,
        )[0]
    else:
        summed = sum([value.astype(F32) for value in sums])
        grad_hidden = jnp.where(
            grid.z < live, hidden_gradient(summed, student_f, student_gain), 0.0
        )
    return (grad_hidden, row_loss[0, :share])


def solution(mesh):
    placed = (
        P("tp", "dp", None),
        P(("dp", "tp"), None),
        P(),
        P(),
        P(None, ("dp", "tp")),
        P(("dp", "tp"), None),
        P(),
        P(None, ("dp", "tp")),
        P("dp"),
        P("dp", None),
    )
    return jax.shard_map(
        shards,
        mesh=mesh,
        in_specs=placed,
        out_specs=(P(("dp", "tp"), None), P(("dp", "tp"))),
        check_vma=False,
    )
```

```python
import functools

import jax
import jax.numpy as jnp
from jax import lax
from jax.experimental import pallas as pl
from jax.experimental.pallas import tpu as pltpu
from jax.sharding import PartitionSpec as P


EPS = 1e-06
BETA = 0.5
LOSS_SCALE = 1024.0
LIVE = 96
PARTS = 2
F32 = jnp.float32
BF16 = jnp.bfloat16
AXES = ("dp", "tp")


class Grid:
    def __init__(self, dp, tp, share):
        assert dp == 4 and tp % 2 == 0
        self.tp, self.depth = tp, tp // 2
        self.live = LIVE // (2 * share)
        assert self.live * 2 * share == LIVE
        dp_at, tp_at = lax.axis_index("dp"), lax.axis_index("tp")
        self.y, self.c = dp_at // 2, dp_at % 2
        self.z, self.x = tp_at // 2, tp_at % 2
        self.tiled = share % 16 == 0
        self.ids = jnp.stack([self.y, self.c, self.z, self.x, dp_at * tp + tp_at])

    def send(self, value, a=0, b=0, k=0, d=0, source=None, target=None):
        pairs = []
        for dp_at in range(4):
            for tp_at in range(self.tp):
                z = tp_at // 2
                if source is not None and z >= source:
                    continue
                if target is not None and (z ^ k) >= target:
                    continue
                to = (dp_at ^ (2 * a + b)) * self.tp + (tp_at ^ (2 * k + d))
                pairs.append((dp_at * self.tp + tp_at, to))
        return lax.ppermute(value, AXES, pairs)

    def send_depth(self, values, source=None, target=None):
        got = []
        for k, value in enumerate(values, 1):
            got.append(self.send(value, k=k, source=source, target=target))
        return got


def pick(pieces, index):
    bit = 0
    while len(pieces) > 1:
        high = (index >> bit) & 1
        pieces = [jnp.where(high == 1, pieces[i + 1], pieces[i]) for i in range(0, len(pieces), 2)]
        bit += 1
    return pieces[0]


def norm_rows(values, gain):
    inverse = lax.rsqrt(jnp.mean(values * values, axis=-1, keepdims=True) + EPS)
    return (values * inverse * gain, inverse)


VMEM = pl.BlockSpec(memory_space=pltpu.VMEM)
SMEM = pl.BlockSpec(memory_space=pltpu.SMEM)
shape_of = pltpu.VMEM
MIB = 1 << 20


def call(kernel, ids, args, outs, scratch, mib, far=()):
    args = [pltpu.with_memory_space_constraint(arg, pltpu.VMEM) for arg in args]
    far = [pltpu.with_memory_space_constraint(arg, pltpu.HBM) for arg in far]
    return pl.pallas_call(
        kernel,
        out_shape=outs,
        in_specs=[SMEM] + [VMEM] * len(args) + [pl.BlockSpec(memory_space=pltpu.HBM)] * len(far),
        out_specs=[VMEM] * len(outs),
        scratch_shapes=scratch,
        compiler_params=pltpu.CompilerParams(vmem_limit_bytes=mib * MIB),
    )(ids, *args, *far)


def pick_kernel(live, count, ids, *refs):
    pieces, outs = refs[:-count], refs[-count:]
    share, width = pieces[0].shape[0], outs[0].shape[1]
    for j in range(live):
        for k, piece in enumerate(pieces):

            @pl.when((ids[2] ^ j) == k)
            def _(j=j, piece=piece):
                for part, out in enumerate(outs):
                    there = slice(part * width, (part + 1) * width)
                    out[j * share : (j + 1) * share, :] = piece[:, there]


def pair_kernel(live, ids, kept, other, own, *lows):
    def chunk(slot):
        slot = jnp.minimum(slot, live - 1)
        return kept[slot].astype(F32) + other[slot].astype(F32)

    own[...] = chunk(ids[2])
    for k, low in enumerate(lows, 1):
        low[...] = chunk(ids[2] ^ k).astype(BF16)


def norm_kernel(ids, *refs):
    own, others = refs[0], refs[1:-4]
    residual, post_gain, final_gain, out = refs[-4:]
    total = own[...]
    for other in others:
        total = total + other[...].astype(F32)
    post, _ = norm_rows(total, post_gain[...])
    final = residual[...].astype(F32) + post
    out[...] = norm_rows(final, final_gain[...])[0].astype(BF16)


def gather_depth(grid, rows, count):
    share, width = rows.shape[0], rows.shape[1] // count
    pieces = [rows] + grid.send_depth([rows] * (grid.depth - 1), source=grid.live)
    if not grid.tiled:
        whole = [pick(pieces, grid.z ^ j) for j in range(grid.live)]
        return jnp.split(jnp.concatenate(whole, axis=0), count, axis=1)
    return call(
        functools.partial(pick_kernel, grid.live, count),
        grid.ids,
        pieces,
        [shape_of((grid.live * share, width), rows.dtype)] * count,
        [],
        4,
    )


def gather_plane(grid, own):
    by_x = grid.send(own, d=1)
    by_y = grid.send(own, a=1)
    far = grid.send(own, a=1, d=1)
    own_c = grid.send(own, b=1)
    by_x_c = grid.send(by_x, b=1)
    by_y_c = grid.send(by_y, b=1)
    far_c = grid.send(far, b=1)
    return jnp.concatenate([own, by_x, own_c, by_x_c, by_y, far, by_y_c, far_c], axis=0)


def lane(shape):
    return lax.broadcasted_iota(jnp.int32, shape, 1)


def own_place(ids):
    return ids[0] * 4 + ids[1] * 2 + ids[3]


def block_rows(number, rows):
    return pl.ds(pl.multiple_of(number * rows, rows), rows)


def student_kernel(ids, logits, labels, cols):
    vocab = logits.shape[1]
    rows = logits.shape[0] // 8
    mine = own_place(ids)

    def step(r, carry):
        here = block_rows(r, rows)
        block = logits[here, :]
        top = jnp.max(block, axis=1, keepdims=True)
        log = top + jnp.log(jnp.sum(jnp.exp(block - top), axis=1, keepdims=True))
        hit = labels[here, :] - ids[4] * vocab == lane(block.shape)
        value = jnp.sum(jnp.where(hit, block, 0.0), axis=1, keepdims=True)
        places = lane((rows, 128))
        cols[block_rows(mine ^ r, rows), :] = jnp.where(
            places == 1, log, jnp.where(places == 3, value, 0.0)
        )
        return carry

    lax.fori_loop(0, 8, step, 0)


def teacher_kernel(ids, logits, s_logits, s_cols, sent, cols):
    rows = logits.shape[0] // 8
    mine = own_place(ids)

    def step(r, carry):
        here = block_rows(r, rows)
        block = logits[here, :]
        top = jnp.max(block, axis=1, keepdims=True)
        weights = jnp.exp(block - top)
        total = jnp.sum(weights, axis=1, keepdims=True)
        mix = jnp.sum(weights * (block - s_logits[here, :]), axis=1, keepdims=True) / total
        places = lane((rows, 128))
        log = top + jnp.log(total)
        there = block_rows(mine ^ r, rows)
        cols[there, :] = jnp.where(
            places == 0, log, jnp.where(places == 2, mix, s_cols[there, :])
        )
        return carry

    lax.fori_loop(0, 8, step, 0, unroll=4)
    turned = cols[...].T
    message = jnp.concatenate([turned[n : n + 1, :] for n in range(4)], axis=1)
    for d in range(sent.shape[0]):
        sent[d] = message


def joined(got, rows):
    every = [got[d][:, : 2 * rows] for d in range(got.shape[0])]
    top = functools.reduce(jnp.maximum, every)
    return top + jnp.log(sum([jnp.exp(part - top) for part in every[1:]], jnp.exp(every[0] - top)))


def logit_kernel(
    ids, got, labels, scale, t_logits, s_logits, kept, grads, lines, columns
):
    vocab = t_logits.shape[1]
    rows = t_logits.shape[0] // 8
    total = joined(got, 8 * rows)
    lines[...] = jnp.zeros_like(lines)
    lines[0:1, :] = total[:, : 8 * rows]
    lines[1:2, :] = total[:, 8 * rows :]
    columns[...] = lines[...].T
    mine = own_place(ids)
    for r in range(8):
        here = slice(r * rows, (r + 1) * rows)
        logs = columns[block_rows(mine ^ r, rows), :]
        t_prob = jnp.exp(t_logits[here, :] - logs[:, 0:1])
        s_prob = jnp.exp(s_logits[here, :] - logs[:, 1:2])
        hit = labels[here, :] - ids[4] * vocab == lane(t_prob.shape)
        grad = scale[here, :] * ((1.0 + BETA) * s_prob - t_prob - BETA * hit.astype(F32))
        place = (r // 4) * 2 + r % 2
        into = grads if (r // 2) % 2 else kept
        into[place * rows : (place + 1) * rows, :] = grad.astype(BF16)


def prep_kernel(live, share, nseq, ids, *refs):
    packed, (labels, scale, weights, turned) = refs[:4], refs[4:]
    tok = turned.shape[0]
    places = lane((1, tok))
    turned[...] = jnp.zeros_like(turned)
    for g, ref in enumerate(packed):
        start = jnp.zeros((1, 1), jnp.int32)
        covered = jnp.zeros((1, tok), jnp.int32)
        spans = jnp.zeros((1, tok), jnp.int32)
        for n in range(nseq):
            length = ref[:, tok + n : tok + n + 1]
            inside = ((places >= start) & (places < start + length)).astype(jnp.int32)
            covered = covered + inside
            spans = spans + inside * length
            start = start + length
        weight = covered.astype(F32) / jnp.maximum(spans, 1).astype(F32)
        if g == 0:
            weights[...] = weight
        turned[g : g + 1, :] = ref[:, :tok].astype(F32)
        turned[4 + g : 5 + g, :] = LOSS_SCALE * weight
    turned[...] = turned[...].T
    for i in range(8):
        g, d = i // 2, i % 2
        for z in range(live):
            there = slice((i * live + z) * share, (i * live + z + 1) * share)
            here = block_rows(2 * z + (ids[3] ^ d), share)
            block = turned[here, :]
            labels[there, :] = block[:, g : g + 1].astype(jnp.int32)
            scale[there, :] = block[:, 4 + g : 5 + g]


def loss_kernel(live, share, ids, got, weights, loss):
    tok = weights.shape[1]
    rows = 8 * live * share
    total = joined(got, rows)
    t_log = total[:, :rows]
    s_log = total[:, rows:]
    cross, value = 0.0, 0.0
    for d in range(got.shape[0]):
        part = got[d]
        cross = cross + jnp.exp(part[:, :rows] - t_log) * part[:, 2 * rows : 3 * rows]
        value = value + part[:, 3 * rows :]
    line = cross - t_log + s_log + BETA * (s_log - value)
    slot = jnp.minimum(ids[2], live - 1)
    at = (own_place(ids) * live + slot) * share
    own = pltpu.roll(line, rows - at, 1)[:, :128]
    weight = pltpu.roll(weights[...], tok - (2 * slot + ids[3]) * share, 1)[:, :128]
    keep = (weight > 0) & (ids[2] < live)
    loss[...] = jnp.where(keep, own, 0.0)


def add_kernel(ids, kept, other, own, *outs):
    rows = own.shape[0]
    own[...] = kept[:rows, :] + other[:rows, :].astype(F32)
    for i, out in enumerate(outs, 1):
        here = slice(i * rows, (i + 1) * rows)
        out[...] = (kept[here, :] + other[here, :].astype(F32)).astype(BF16)


def chunk_kernel(live, ids, *refs):
    parts, (own, *lows) = refs[: 4 * PARTS], refs[4 * PARTS :]
    share, width = own.shape[0], own.shape[1] // PARTS

    def chunk(out, slot):
        here = block_rows(jnp.minimum(slot, live - 1), share)
        for part in range(PARTS):
            base, by_x, by_y, far = parts[4 * part : 4 * part + 4]
            total = base[here, :] + by_x[here, :].astype(F32)
            total = total + by_y[here, :].astype(F32) + far[here, :].astype(F32)
            out[:, part * width : (part + 1) * width] = total.astype(out.dtype)

    chunk(own, ids[2])
    for k, low in enumerate(lows, 1):
        chunk(low, ids[2] ^ k)


def final_kernel(live, ids, own, *refs):
    chunks, (hidden, gain, out) = refs[:-3], refs[-3:]
    summed = own[...]
    for chunk in chunks:
        summed = summed + chunk[...].astype(F32)
    out[...] = hidden_gradient(summed, hidden[...].astype(F32), gain[...])

    @pl.when(ids[2] >= live)
    def _():
        out[...] = jnp.zeros_like(out)


def hidden_gradient(summed, hidden, gain):
    inverse = lax.rsqrt(jnp.mean(hidden * hidden, axis=-1, keepdims=True) + EPS)
    scaled = summed * gain
    inner = jnp.mean(scaled * hidden, axis=1, keepdims=True)
    return inverse * scaled - hidden * (inverse * inverse * inverse) * inner


def product(grads, head, part, dtype):
    width = head.shape[0] // PARTS
    return lax.dot_general(
        grads,
        head[part * width : (part + 1) * width],
        (((1,), (1,)), ((), ())),
        preferred_element_type=F32,
    ).astype(dtype)


def reduce_plane(grid, kept, other):
    rows, width = kept.shape[0] // 4, kept.shape[1]
    own, to_x, to_y, to_far = call(
        add_kernel,
        grid.ids,
        [kept, other],
        [shape_of((rows, width), F32)] + [shape_of((rows, width), BF16)] * 3,
        [],
        4,
    )
    return own, grid.send(to_x, d=1), grid.send(to_y, a=1), grid.send(to_far, a=1, d=1)


def reduce_depth(grid, parts, share):
    width = PARTS * parts[0][0].shape[1]
    if grid.tiled:
        summed, *lows = call(
            functools.partial(chunk_kernel, grid.live),
            grid.ids,
            [value for part in parts for value in part],
            [shape_of((share, width), F32)] + [shape_of((share, width), BF16)] * (grid.depth - 1),
            [],
            4,
        )
    else:
        mine = jnp.concatenate([sum([value.astype(F32) for value in part]) for part in parts], axis=1)
        mine = mine.reshape(grid.live, share, width)
        slots = [jnp.minimum(grid.z ^ k, grid.live - 1) for k in range(grid.depth)]
        summed, *lows = [lax.dynamic_index_in_dim(mine, k, 0, keepdims=False) for k in slots]
        lows = [low.astype(BF16) for low in lows]
    return [summed] + grid.send_depth(lows, target=grid.live)


def row_weights(lengths, tok_rows):
    ends = jnp.cumsum(lengths, axis=1)
    starts = ends - lengths
    places = jnp.arange(tok_rows, dtype=jnp.int32)
    inside = (places[None, :, None] >= starts[:, None, :]) & (
        places[None, :, None] < ends[:, None, :]
    )
    spans = jnp.sum(jnp.where(inside, lengths[:, None, :], 0), axis=2)
    covered = jnp.sum(inside.astype(jnp.int32), axis=2)
    return covered.astype(F32) / jnp.maximum(spans, 1).astype(F32)


def shards(
    teacher_partial,
    teacher_residual,
    post_gain,
    final_gain,
    teacher_head,
    student_hidden,
    student_gain,
    student_head,
    labels,
    lengths,
):
    share, width_t = teacher_residual.shape
    width_s = student_hidden.shape[1]
    tok_rows = labels.shape[0]
    nseq = lengths.shape[1]
    grid = Grid(lax.axis_size("dp"), lax.axis_size("tp"), share)
    live = grid.live

    zero = jnp.zeros((), jnp.int32)
    parts = teacher_partial.reshape(-1, 2, share, width_t)

    def half_of(x):
        begin = (zero, x, zero, zero)
        rows = lax.dynamic_slice(parts, begin, (live, 1, share, width_t))
        return rows.reshape(live, share, width_t)

    given = half_of(1 - grid.x)
    kept = half_of(grid.x)
    other = grid.send(given, d=1)
    at = jnp.minimum(grid.z, live - 1)
    ks = range(1, grid.depth)
    if grid.tiled:
        own, *lows = call(
            functools.partial(pair_kernel, live),
            grid.ids,
            [kept, other],
            [shape_of((share, width_t), F32)] + [shape_of((share, width_t), BF16) for k in ks],
            [],
            4,
        )
    else:
        pair = kept.astype(F32) + other.astype(F32)
        own = lax.dynamic_index_in_dim(pair, at, 0, keepdims=False)
        lows = [
            lax.dynamic_index_in_dim(
                pair, jnp.minimum(grid.z ^ k, live - 1), 0, keepdims=False
            ).astype(BF16)
            for k in ks
        ]
    others = grid.send_depth(lows, target=live)

    student_f = student_hidden.astype(F32)
    student_norm = norm_rows(student_f, student_gain)[0].astype(BF16)
    own_s = gather_depth(grid, student_norm, 1)[0]
    whole_s = gather_plane(grid, own_s)

    ints = jnp.concatenate([labels, lengths[0]])[None]
    packed = [ints] + [grid.send(ints, a=a, b=b) for a, b in ((0, 1), (1, 0), (1, 1))]

    def by_row(value):
        value = value[:, :LIVE].reshape(4, live, 2, share)
        value = jnp.moveaxis(value, 2, 1)
        value = jnp.where(grid.x == 1, jnp.flip(value, 1), value)
        return value.reshape(-1)[:, None]

    rows = 8 * live * share
    if grid.tiled:
        label_column, scale_column, weight_line = call(
            functools.partial(prep_kernel, live, share, nseq),
            grid.ids,
            packed,
            [
                shape_of((rows, 1), jnp.int32),
                shape_of((rows, 1), F32),
                shape_of((1, tok_rows), F32),
            ],
            [pltpu.VMEM((tok_rows, 128), F32)],
            4,
        )
    else:
        whole = jnp.concatenate(packed, axis=0)
        weight_rows = row_weights(whole[:, tok_rows : tok_rows + nseq], tok_rows)
        label_column = by_row(whole[:, :tok_rows])
        scale_column = by_row(LOSS_SCALE * weight_rows)
        weight_line = weight_rows[:1]

    if grid.tiled:
        teacher_norm = call(
            norm_kernel,
            grid.ids,
            [own, *others, teacher_residual, post_gain[None], final_gain[None]],
            [shape_of((share, width_t), BF16)],
            [],
            4,
        )[0]
    else:
        mlp_sum = own
        for other in others:
            mlp_sum = mlp_sum + other.astype(F32)
        post, _ = norm_rows(mlp_sum, post_gain)
        final = teacher_residual.astype(F32) + post
        teacher_norm = norm_rows(final, final_gain)[0].astype(BF16)
    own_t = gather_depth(grid, teacher_norm, PARTS)
    whole_t = [gather_plane(grid, part) for part in own_t]

    vocab_dev = student_head.shape[1]

    s_logits = jnp.dot(whole_s, student_head, preferred_element_type=F32)
    s_cols = call(
        student_kernel, grid.ids, [s_logits, label_column], [shape_of((rows, 128), F32)], [], 4
    )[0]
    t_logits = 0.0
    for i, part in enumerate(whole_t):
        width = part.shape[1]
        t_logits = t_logits + jnp.dot(
            part, teacher_head[i * width : (i + 1) * width], preferred_element_type=F32
        )
        if i < PARTS - 1:
            t_logits = lax.optimization_barrier(t_logits)
    devices = 4 * grid.tp
    sent = call(
        teacher_kernel,
        grid.ids,
        [t_logits, s_logits, s_cols],
        [shape_of((devices, 1, 4 * rows), F32)],
        [pltpu.VMEM((rows, 128), F32)],
        8,
    )[0]
    got = lax.all_to_all(sent, AXES, 0, 0, tiled=True)

    half = rows // 2
    keeps, gives = call(
        logit_kernel,
        grid.ids,
        [got, label_column, scale_column, t_logits, s_logits],
        [shape_of((half, vocab_dev), BF16), shape_of((half, vocab_dev), BF16)],
        [pltpu.VMEM((128, rows), F32), pltpu.VMEM((rows, 128), F32)],
        6,
    )
    others = []
    for part in range(PARTS):
        given = product(gives, student_head, part, BF16)
        others.append(grid.send(given, b=1))
    parts = []
    for part in range(PARTS):
        kept = product(keeps, student_head, part, F32)
        parts.append(reduce_plane(grid, kept, others[part]))
    sums = reduce_depth(grid, parts, share)
    row_loss = call(
        functools.partial(loss_kernel, live, share),
        grid.ids,
        [got, weight_line],
        [shape_of((1, 128), F32)],
        [],
        4,
    )[0]
    if grid.tiled:
        grad_hidden = call(
            functools.partial(final_kernel, live),
            grid.ids,
            [*sums, student_hidden, student_gain[None]],
            [jax.ShapeDtypeStruct((share, width_s), F32)],
            [],
            4,
        )[0]
    else:
        summed = sum([value.astype(F32) for value in sums])
        grad_hidden = jnp.where(
            grid.z < live, hidden_gradient(summed, student_f, student_gain), 0.0
        )
    return (grad_hidden, row_loss[0, :share])


def solution(mesh):
    placed = (
        P("tp", "dp", None),
        P(("dp", "tp"), None),
        P(),
        P(),
        P(None, ("dp", "tp")),
        P(("dp", "tp"), None),
        P(),
        P(None, ("dp", "tp")),
        P("dp"),
        P("dp", None),
    )
    return jax.shard_map(
        shards,
        mesh=mesh,
        in_specs=placed,
        out_specs=(P(("dp", "tp"), None), P(("dp", "tp"))),
        check_vma=False,
    )
```

```python
import functools

import jax
import jax.numpy as jnp
from jax import lax
from jax.experimental import pallas as pl
from jax.experimental.pallas import tpu as pltpu
from jax.sharding import PartitionSpec as P


EPS = 1e-06
BETA = 0.5
LOSS_SCALE = 1024.0
LIVE = 96
PARTS = 2
F32 = jnp.float32
BF16 = jnp.bfloat16
AXES = ("dp", "tp")


class Grid:
    def __init__(self, dp, tp, share):
        assert dp == 4 and tp % 2 == 0
        self.tp, self.depth = tp, tp // 2
        self.live = LIVE // (2 * share)
        assert self.live * 2 * share == LIVE
        dp_at, tp_at = lax.axis_index("dp"), lax.axis_index("tp")
        self.y, self.c = dp_at // 2, dp_at % 2
        self.z, self.x = tp_at // 2, tp_at % 2
        self.tiled = share % 16 == 0
        self.ids = jnp.stack([self.y, self.c, self.z, self.x, dp_at * tp + tp_at])

    def send(self, value, a=0, b=0, k=0, d=0, source=None, target=None):
        pairs = []
        for dp_at in range(4):
            for tp_at in range(self.tp):
                z = tp_at // 2
                if source is not None and z >= source:
                    continue
                if target is not None and (z ^ k) >= target:
                    continue
                to = (dp_at ^ (2 * a + b)) * self.tp + (tp_at ^ (2 * k + d))
                pairs.append((dp_at * self.tp + tp_at, to))
        return lax.ppermute(value, AXES, pairs)

    def send_depth(self, values, source=None, target=None):
        got = []
        for k, value in enumerate(values, 1):
            got.append(self.send(value, k=k, source=source, target=target))
        return got


def pick(pieces, index):
    bit = 0
    while len(pieces) > 1:
        high = (index >> bit) & 1
        pieces = [jnp.where(high == 1, pieces[i + 1], pieces[i]) for i in range(0, len(pieces), 2)]
        bit += 1
    return pieces[0]


def norm_rows(values, gain):
    inverse = lax.rsqrt(jnp.mean(values * values, axis=-1, keepdims=True) + EPS)
    return (values * inverse * gain, inverse)


VMEM = pl.BlockSpec(memory_space=pltpu.VMEM)
SMEM = pl.BlockSpec(memory_space=pltpu.SMEM)
shape_of = pltpu.VMEM
MIB = 1 << 20


def call(kernel, ids, args, outs, scratch, mib, far=()):
    args = [pltpu.with_memory_space_constraint(arg, pltpu.VMEM) for arg in args]
    far = [pltpu.with_memory_space_constraint(arg, pltpu.HBM) for arg in far]
    return pl.pallas_call(
        kernel,
        out_shape=outs,
        in_specs=[SMEM] + [VMEM] * len(args) + [pl.BlockSpec(memory_space=pltpu.HBM)] * len(far),
        out_specs=[VMEM] * len(outs),
        scratch_shapes=scratch,
        compiler_params=pltpu.CompilerParams(vmem_limit_bytes=mib * MIB),
    )(ids, *args, *far)


def pick_kernel(live, count, ids, *refs):
    pieces, outs = refs[:-count], refs[-count:]
    share, width = pieces[0].shape[0], outs[0].shape[1]
    for j in range(live):
        for k, piece in enumerate(pieces):

            @pl.when((ids[2] ^ j) == k)
            def _(j=j, piece=piece):
                for part, out in enumerate(outs):
                    there = slice(part * width, (part + 1) * width)
                    out[j * share : (j + 1) * share, :] = piece[:, there]


def pair_kernel(live, ids, kept, other, own, *lows):
    def chunk(slot):
        slot = jnp.minimum(slot, live - 1)
        return kept[slot].astype(F32) + other[slot].astype(F32)

    own[...] = chunk(ids[2])
    for k, low in enumerate(lows, 1):
        low[...] = chunk(ids[2] ^ k).astype(BF16)


def norm_kernel(ids, *refs):
    own, others = refs[0], refs[1:-4]
    residual, post_gain, final_gain, out = refs[-4:]
    total = own[...]
    for other in others:
        total = total + other[...].astype(F32)
    post, _ = norm_rows(total, post_gain[...])
    final = residual[...].astype(F32) + post
    out[...] = norm_rows(final, final_gain[...])[0].astype(BF16)


def gather_depth(grid, rows, count):
    share, width = rows.shape[0], rows.shape[1] // count
    pieces = [rows] + grid.send_depth([rows] * (grid.depth - 1), source=grid.live)
    if not grid.tiled:
        whole = [pick(pieces, grid.z ^ j) for j in range(grid.live)]
        return jnp.split(jnp.concatenate(whole, axis=0), count, axis=1)
    return call(
        functools.partial(pick_kernel, grid.live, count),
        grid.ids,
        pieces,
        [shape_of((grid.live * share, width), rows.dtype)] * count,
        [],
        4,
    )


def gather_plane(grid, own):
    by_x = grid.send(own, d=1)
    by_y = grid.send(own, a=1)
    far = grid.send(own, a=1, d=1)
    own_c = grid.send(own, b=1)
    by_x_c = grid.send(by_x, b=1)
    by_y_c = grid.send(by_y, b=1)
    far_c = grid.send(far, b=1)
    return jnp.concatenate([own, by_x, own_c, by_x_c, by_y, far, by_y_c, far_c], axis=0)


def lane(shape):
    return lax.broadcasted_iota(jnp.int32, shape, 1)


def own_place(ids):
    return ids[0] * 4 + ids[1] * 2 + ids[3]


def block_rows(number, rows):
    return pl.ds(pl.multiple_of(number * rows, rows), rows)


def student_kernel(ids, logits, labels, cols):
    vocab = logits.shape[1]
    rows = logits.shape[0] // 8
    mine = own_place(ids)

    def step(r, carry):
        here = block_rows(r, rows)
        block = logits[here, :]
        top = jnp.max(block, axis=1, keepdims=True)
        log = top + jnp.log(jnp.sum(jnp.exp(block - top), axis=1, keepdims=True))
        hit = labels[here, :] - ids[4] * vocab == lane(block.shape)
        value = jnp.sum(jnp.where(hit, block, 0.0), axis=1, keepdims=True)
        places = lane((rows, 128))
        cols[block_rows(mine ^ r, rows), :] = jnp.where(
            places == 1, log, jnp.where(places == 3, value, 0.0)
        )
        return carry

    lax.fori_loop(0, 8, step, 0)


def teacher_kernel(ids, logits, s_logits, s_cols, sent, cols):
    rows = logits.shape[0] // 8
    mine = own_place(ids)

    def step(r, carry):
        here = block_rows(r, rows)
        block = logits[here, :]
        top = jnp.max(block, axis=1, keepdims=True)
        weights = jnp.exp(block - top)
        total = jnp.sum(weights, axis=1, keepdims=True)
        mix = jnp.sum(weights * (block - s_logits[here, :]), axis=1, keepdims=True) / total
        places = lane((rows, 128))
        log = top + jnp.log(total)
        there = block_rows(mine ^ r, rows)
        cols[there, :] = jnp.where(
            places == 0, log, jnp.where(places == 2, mix, s_cols[there, :])
        )
        return carry

    lax.fori_loop(0, 8, step, 0, unroll=4)
    turned = cols[...].T
    message = jnp.concatenate([turned[n : n + 1, :] for n in range(4)], axis=1)
    for d in range(sent.shape[0]):
        sent[d] = message


def joined(got, rows):
    every = [got[d][:, : 2 * rows] for d in range(got.shape[0])]
    top = functools.reduce(jnp.maximum, every)
    return top + jnp.log(sum([jnp.exp(part - top) for part in every[1:]], jnp.exp(every[0] - top)))


def logit_kernel(
    ids, got, labels, scale, t_logits, s_logits, kept, grads, lines, columns
):
    vocab = t_logits.shape[1]
    rows = t_logits.shape[0] // 8
    total = joined(got, 8 * rows)
    lines[...] = jnp.zeros_like(lines)
    lines[0:1, :] = total[:, : 8 * rows]
    lines[1:2, :] = total[:, 8 * rows :]
    columns[...] = lines[...].T
    mine = own_place(ids)
    for r in range(8):
        here = slice(r * rows, (r + 1) * rows)
        logs = columns[block_rows(mine ^ r, rows), :]
        t_prob = jnp.exp(t_logits[here, :] - logs[:, 0:1])
        s_prob = jnp.exp(s_logits[here, :] - logs[:, 1:2])
        hit = labels[here, :] - ids[4] * vocab == lane(t_prob.shape)
        grad = scale[here, :] * ((1.0 + BETA) * s_prob - t_prob - BETA * hit.astype(F32))
        place = (r // 4) * 2 + r % 2
        into = grads if (r // 2) % 2 else kept
        into[place * rows : (place + 1) * rows, :] = grad.astype(BF16)


def prep_kernel(live, share, nseq, ids, *refs):
    packed, (labels, scale, weights, turned) = refs[:4], refs[4:]
    tok = turned.shape[0]
    places = lane((1, tok))
    turned[...] = jnp.zeros_like(turned)
    for g, ref in enumerate(packed):
        start = jnp.zeros((1, 1), jnp.int32)
        covered = jnp.zeros((1, tok), jnp.int32)
        spans = jnp.zeros((1, tok), jnp.int32)
        for n in range(nseq):
            length = ref[:, tok + n : tok + n + 1]
            inside = ((places >= start) & (places < start + length)).astype(jnp.int32)
            covered = covered + inside
            spans = spans + inside * length
            start = start + length
        weight = covered.astype(F32) / jnp.maximum(spans, 1).astype(F32)
        if g == 0:
            weights[...] = weight
        turned[g : g + 1, :] = ref[:, :tok].astype(F32)
        turned[4 + g : 5 + g, :] = LOSS_SCALE * weight
    turned[...] = turned[...].T
    for i in range(8):
        g, d = i // 2, i % 2
        for z in range(live):
            there = slice((i * live + z) * share, (i * live + z + 1) * share)
            here = block_rows(2 * z + (ids[3] ^ d), share)
            block = turned[here, :]
            labels[there, :] = block[:, g : g + 1].astype(jnp.int32)
            scale[there, :] = block[:, 4 + g : 5 + g]


def loss_kernel(live, share, ids, got, weights, loss):
    tok = weights.shape[1]
    rows = 8 * live * share
    total = joined(got, rows)
    t_log = total[:, :rows]
    s_log = total[:, rows:]
    cross, value = 0.0, 0.0
    for d in range(got.shape[0]):
        part = got[d]
        cross = cross + jnp.exp(part[:, :rows] - t_log) * part[:, 2 * rows : 3 * rows]
        value = value + part[:, 3 * rows :]
    line = cross - t_log + s_log + BETA * (s_log - value)
    slot = jnp.minimum(ids[2], live - 1)
    at = (own_place(ids) * live + slot) * share
    own = pltpu.roll(line, rows - at, 1)[:, :128]
    weight = pltpu.roll(weights[...], tok - (2 * slot + ids[3]) * share, 1)[:, :128]
    keep = (weight > 0) & (ids[2] < live)
    loss[...] = jnp.where(keep, own, 0.0)


def add_kernel(ids, kept, other, own, *outs):
    rows = own.shape[0]
    own[...] = kept[:rows, :] + other[:rows, :].astype(F32)
    for i, out in enumerate(outs, 1):
        here = slice(i * rows, (i + 1) * rows)
        out[...] = (kept[here, :] + other[here, :].astype(F32)).astype(BF16)


def chunk_kernel(live, ids, *refs):
    parts, (own, *lows) = refs[: 4 * PARTS], refs[4 * PARTS :]
    share = own.shape[0]

    def chunk(out, slot):
        here = block_rows(jnp.minimum(slot, live - 1), share)
        begin = 0
        for part in range(PARTS):
            base, by_x, by_y, far = parts[4 * part : 4 * part + 4]
            total = base[here, :] + by_x[here, :].astype(F32)
            total = total + by_y[here, :].astype(F32) + far[here, :].astype(F32)
            end = begin + base.shape[1]
            out[:, begin:end] = total.astype(out.dtype)
            begin = end

    chunk(own, ids[2])
    for k, low in enumerate(lows, 1):
        chunk(low, ids[2] ^ k)


def final_kernel(live, ids, own, *refs):
    chunks, (hidden, gain, out) = refs[:-3], refs[-3:]
    summed = own[...]
    for chunk in chunks:
        summed = summed + chunk[...].astype(F32)
    out[...] = hidden_gradient(summed, hidden[...].astype(F32), gain[...])

    @pl.when(ids[2] >= live)
    def _():
        out[...] = jnp.zeros_like(out)


def hidden_gradient(summed, hidden, gain):
    inverse = lax.rsqrt(jnp.mean(hidden * hidden, axis=-1, keepdims=True) + EPS)
    scaled = summed * gain
    inner = jnp.mean(scaled * hidden, axis=1, keepdims=True)
    return inverse * scaled - hidden * (inverse * inverse * inverse) * inner


def product(grads, head, part, dtype):
    cut = head.shape[0] * 4 // 7 // 128 * 128
    return lax.dot_general(
        grads,
        head[cut:] if part else head[:cut],
        (((1,), (1,)), ((), ())),
        preferred_element_type=F32,
    ).astype(dtype)


def reduce_plane(grid, kept, other):
    rows, width = kept.shape[0] // 4, kept.shape[1]
    own, to_x, to_y, to_far = call(
        add_kernel,
        grid.ids,
        [kept, other],
        [shape_of((rows, width), F32)] + [shape_of((rows, width), BF16)] * 3,
        [],
        4,
    )
    return own, grid.send(to_x, d=1), grid.send(to_y, a=1), grid.send(to_far, a=1, d=1)


def reduce_depth(grid, parts, share):
    width = sum([part[0].shape[1] for part in parts])
    if grid.tiled:
        summed, *lows = call(
            functools.partial(chunk_kernel, grid.live),
            grid.ids,
            [value for part in parts for value in part],
            [shape_of((share, width), F32)] + [shape_of((share, width), BF16)] * (grid.depth - 1),
            [],
            4,
        )
    else:
        mine = jnp.concatenate([sum([value.astype(F32) for value in part]) for part in parts], axis=1)
        mine = mine.reshape(grid.live, share, width)
        slots = [jnp.minimum(grid.z ^ k, grid.live - 1) for k in range(grid.depth)]
        summed, *lows = [lax.dynamic_index_in_dim(mine, k, 0, keepdims=False) for k in slots]
        lows = [low.astype(BF16) for low in lows]
    return [summed] + grid.send_depth(lows, target=grid.live)


def row_weights(lengths, tok_rows):
    ends = jnp.cumsum(lengths, axis=1)
    starts = ends - lengths
    places = jnp.arange(tok_rows, dtype=jnp.int32)
    inside = (places[None, :, None] >= starts[:, None, :]) & (
        places[None, :, None] < ends[:, None, :]
    )
    spans = jnp.sum(jnp.where(inside, lengths[:, None, :], 0), axis=2)
    covered = jnp.sum(inside.astype(jnp.int32), axis=2)
    return covered.astype(F32) / jnp.maximum(spans, 1).astype(F32)


def shards(
    teacher_partial,
    teacher_residual,
    post_gain,
    final_gain,
    teacher_head,
    student_hidden,
    student_gain,
    student_head,
    labels,
    lengths,
):
    share, width_t = teacher_residual.shape
    width_s = student_hidden.shape[1]
    tok_rows = labels.shape[0]
    nseq = lengths.shape[1]
    grid = Grid(lax.axis_size("dp"), lax.axis_size("tp"), share)
    live = grid.live

    zero = jnp.zeros((), jnp.int32)
    parts = teacher_partial.reshape(-1, 2, share, width_t)

    def half_of(x):
        begin = (zero, x, zero, zero)
        rows = lax.dynamic_slice(parts, begin, (live, 1, share, width_t))
        return rows.reshape(live, share, width_t)

    given = half_of(1 - grid.x)
    kept = half_of(grid.x)
    other = grid.send(given, d=1)
    at = jnp.minimum(grid.z, live - 1)
    ks = range(1, grid.depth)
    if grid.tiled:
        own, *lows = call(
            functools.partial(pair_kernel, live),
            grid.ids,
            [kept, other],
            [shape_of((share, width_t), F32)] + [shape_of((share, width_t), BF16) for k in ks],
            [],
            4,
        )
    else:
        pair = kept.astype(F32) + other.astype(F32)
        own = lax.dynamic_index_in_dim(pair, at, 0, keepdims=False)
        lows = [
            lax.dynamic_index_in_dim(
                pair, jnp.minimum(grid.z ^ k, live - 1), 0, keepdims=False
            ).astype(BF16)
            for k in ks
        ]
    others = grid.send_depth(lows, target=live)

    student_f = student_hidden.astype(F32)
    student_norm = norm_rows(student_f, student_gain)[0].astype(BF16)
    own_s = gather_depth(grid, student_norm, 1)[0]
    whole_s = gather_plane(grid, own_s)

    ints = jnp.concatenate([labels, lengths[0]])[None]
    packed = [ints] + [grid.send(ints, a=a, b=b) for a, b in ((0, 1), (1, 0), (1, 1))]

    def by_row(value):
        value = value[:, :LIVE].reshape(4, live, 2, share)
        value = jnp.moveaxis(value, 2, 1)
        value = jnp.where(grid.x == 1, jnp.flip(value, 1), value)
        return value.reshape(-1)[:, None]

    rows = 8 * live * share
    if grid.tiled:
        label_column, scale_column, weight_line = call(
            functools.partial(prep_kernel, live, share, nseq),
            grid.ids,
            packed,
            [
                shape_of((rows, 1), jnp.int32),
                shape_of((rows, 1), F32),
                shape_of((1, tok_rows), F32),
            ],
            [pltpu.VMEM((tok_rows, 128), F32)],
            4,
        )
    else:
        whole = jnp.concatenate(packed, axis=0)
        weight_rows = row_weights(whole[:, tok_rows : tok_rows + nseq], tok_rows)
        label_column = by_row(whole[:, :tok_rows])
        scale_column = by_row(LOSS_SCALE * weight_rows)
        weight_line = weight_rows[:1]

    if grid.tiled:
        teacher_norm = call(
            norm_kernel,
            grid.ids,
            [own, *others, teacher_residual, post_gain[None], final_gain[None]],
            [shape_of((share, width_t), BF16)],
            [],
            4,
        )[0]
    else:
        mlp_sum = own
        for other in others:
            mlp_sum = mlp_sum + other.astype(F32)
        post, _ = norm_rows(mlp_sum, post_gain)
        final = teacher_residual.astype(F32) + post
        teacher_norm = norm_rows(final, final_gain)[0].astype(BF16)
    own_t = gather_depth(grid, teacher_norm, PARTS)
    whole_t = [gather_plane(grid, part) for part in own_t]

    vocab_dev = student_head.shape[1]

    s_logits = jnp.dot(whole_s, student_head, preferred_element_type=F32)
    s_cols = call(
        student_kernel, grid.ids, [s_logits, label_column], [shape_of((rows, 128), F32)], [], 4
    )[0]
    t_logits = 0.0
    for i, part in enumerate(whole_t):
        width = part.shape[1]
        t_logits = t_logits + jnp.dot(
            part, teacher_head[i * width : (i + 1) * width], preferred_element_type=F32
        )
        if i < PARTS - 1:
            t_logits = lax.optimization_barrier(t_logits)
    devices = 4 * grid.tp
    sent = call(
        teacher_kernel,
        grid.ids,
        [t_logits, s_logits, s_cols],
        [shape_of((devices, 1, 4 * rows), F32)],
        [pltpu.VMEM((rows, 128), F32)],
        8,
    )[0]
    got = lax.all_to_all(sent, AXES, 0, 0, tiled=True)

    half = rows // 2
    keeps, gives = call(
        logit_kernel,
        grid.ids,
        [got, label_column, scale_column, t_logits, s_logits],
        [shape_of((half, vocab_dev), BF16), shape_of((half, vocab_dev), BF16)],
        [pltpu.VMEM((128, rows), F32), pltpu.VMEM((rows, 128), F32)],
        6,
    )
    others = []
    for part in range(PARTS):
        given = product(gives, student_head, part, BF16)
        others.append(grid.send(given, b=1))
    parts = []
    for part in range(PARTS):
        kept = product(keeps, student_head, part, F32)
        parts.append(reduce_plane(grid, kept, others[part]))
    sums = reduce_depth(grid, parts, share)
    row_loss = call(
        functools.partial(loss_kernel, live, share),
        grid.ids,
        [got, weight_line],
        [shape_of((1, 128), F32)],
        [],
        4,
    )[0]
    if grid.tiled:
        grad_hidden = call(
            functools.partial(final_kernel, live),
            grid.ids,
            [*sums, student_hidden, student_gain[None]],
            [jax.ShapeDtypeStruct((share, width_s), F32)],
            [],
            4,
        )[0]
    else:
        summed = sum([value.astype(F32) for value in sums])
        grad_hidden = jnp.where(
            grid.z < live, hidden_gradient(summed, student_f, student_gain), 0.0
        )
    return (grad_hidden, row_loss[0, :share])


def solution(mesh):
    placed = (
        P("tp", "dp", None),
        P(("dp", "tp"), None),
        P(),
        P(),
        P(None, ("dp", "tp")),
        P(("dp", "tp"), None),
        P(),
        P(None, ("dp", "tp")),
        P("dp"),
        P("dp", None),
    )
    return jax.shard_map(
        shards,
        mesh=mesh,
        in_specs=placed,
        out_specs=(P(("dp", "tp"), None), P(("dp", "tp"))),
        check_vma=False,
    )
```
